512 devices in a mesh: seq: 64 (over x, y, core), head: 8 (over z).
Axes of the slice: x: 4, y: 8, z: 8, core: 2. Of those that a mesh axis runs over, the one named last changes fastest.
Arguments:
- text_rows: bfloat16 [8192, 4096], P('seq', 'head'), may hold values from -6 to 6
- picture_rows: bfloat16 [2048, 4096], P('seq', 'head'), may hold values from -6 to 6
- picture_slots: int32 [2048], P('seq'), may hold values from 0 to 8191, as said below
- norm_gain: float32 [4096], replicated, may hold values from 0.1 to 1.9
- w_query: bfloat16 [4096, 4096], P('seq', 'head'), may hold values from -1 to 1
- w_key: bfloat16 [4096, 1024], P('seq', 'head'), may hold values from -1 to 1
- w_value: bfloat16 [4096, 1024], P('seq', 'head'), may hold values from -0.09375 to 0.09375
- w_out: bfloat16 [4096, 4096], P('head', 'seq'), may hold values from -0.5 to 0.5
- cache_keys: bfloat16 [4096, 1024], P('seq', 'head'), may hold values from -500 to 500
- cache_values: bfloat16 [4096, 1024], P('seq', 'head'), may hold values from -6 to 6
- recompute_rows: bfloat16 [512, 4096], P('seq', 'head'), may hold values from -6 to 6
- recompute_slots: int32 [512], P('seq'), may hold values from 0 to 4095, as said below
Outputs:
- mixed: bfloat16 [8192, 4096], P('seq', 'head')
The draws below stay inside these ranges and needn't reach their ends.
Inputs may be any that keep to these rules, and one draw needn't show every extreme that they name: `picture_slots`: distinct stream positions, in runs of 256 consecutive positions, one run a tile; the first tile's run starts at position 4096 and the last tile's run ends at the stream's last position. `recompute_slots`: each aligned block b of 8 entries names distinct rows of cache rows b * 64 to (b + 1) * 64 - 1.
All inputs are finite; a program needn't handle non-finite values.
Results may differ from the reference program's by a relative error of at most 0.02.
Values may be sent and summed in bfloat16 or wider, within the bound.
A program may use at most 128 MiB of HBM per device.

```python
import jax
import jax.numpy as jnp
from jax import lax

D = 4096
HEADS = 32
KV_HEADS = 8
HD = 128
PIC_RUN = 256
CACHE_DEV = 64
REC_DEV = 8
STREAM = 8192
PICS = 2048
CACHE = 4096
RECOMP = 512


def place_runs(key, count, seg_start, seg_len):
    spare = seg_len - count * PIC_RUN
    offsets = jnp.sort(jax.random.randint(key, (count,), 0, spare + 1))
    return (seg_start + offsets + PIC_RUN * jnp.arange(count, dtype=jnp.int32)).astype(jnp.int32)


def draw_picture_slots(key, part):
    tiles = PICS // PIC_RUN
    middle = STREAM // 2
    inner = tiles - 2
    before = inner // 2
    after = inner - before
    first_runs = place_runs(jax.random.fold_in(key, 3), before, 0, middle)
    second_runs = place_runs(jax.random.fold_in(key, 4), after, middle + PIC_RUN, STREAM - middle - 2 * PIC_RUN)
    starts = jnp.concatenate([jnp.array([middle], jnp.int32), first_runs, second_runs, jnp.array([STREAM - PIC_RUN], jnp.int32)])
    return (starts[:, None] + jnp.arange(PIC_RUN, dtype=jnp.int32)[None, :]).reshape(-1).astype(jnp.int32)


def recompute_choice(key):
    blocks = RECOMP // REC_DEV
    subkeys = jax.random.split(jax.random.fold_in(key, 7), blocks)
    chosen = jax.vmap(lambda sub: jax.random.permutation(sub, CACHE_DEV)[:REC_DEV])(subkeys)
    offsets = CACHE_DEV * jnp.arange(blocks, dtype=jnp.int32)
    return (chosen.astype(jnp.int32) + offsets[:, None]).reshape(-1).astype(jnp.int32)


def draw_recompute_slots(key, part):
    return recompute_choice(key)


def weight_table(key, fan_in, columns, tag):
    raw = jax.random.normal(jax.random.fold_in(key, tag), (fan_in, columns), jnp.float32)
    return jnp.clip(raw, -6.0, 6.0) * fan_in ** (-0.5)


def draw_w_query(key, part):
    return weight_table(key, D, HEADS * HD, 21).astype(jnp.bfloat16)


def draw_w_key(key, part):
    return weight_table(key, D, KV_HEADS * HD, 22).astype(jnp.bfloat16)


def draw_picture_rows(key, part):
    noise = jnp.clip(jax.random.normal(jax.random.fold_in(key, 31), (PICS, D), jnp.float32), -6.0, 6.0)
    return noise.astype(jnp.bfloat16)


def draw_cache_keys(key, part):
    base = jnp.clip(jax.random.normal(jax.random.fold_in(key, 11), (CACHE, KV_HEADS * HD), jnp.float32), -6.0, 6.0)
    return base.astype(jnp.bfloat16)


def block_levels(stream_key, extent, cuts, low, top_value):
    def one(axis_at, shards_of):
        steps = jax.random.uniform(jax.random.fold_in(jax.random.fold_in(stream_key, 6), axis_at), (shards_of,), jnp.float32, low / len(cuts), top_value / len(cuts))
        return jnp.repeat(jnp.exp(steps), extent[axis_at] // shards_of).reshape((-1,) + (1,) * (len(extent) - axis_at - 1))

    level = one(*cuts[0])
    for cut in cuts[1:]:
        level = level * one(*cut)
    return level


def normal_values(own_key, dims, spread, reach, shards=(), kind=jnp.bfloat16):
    loudness = block_levels(own_key, dims, shards, -0.22, 0.18) if shards else 1.0
    entries = jax.random.normal(own_key, dims, jnp.float32) * spread * loudness
    return jnp.minimum(jnp.maximum(entries, -reach), reach).astype(kind)


def setup_inputs(seed: int = 0) -> dict:
    key_of = jax.random.split(jax.random.key(seed), 13)
    return {
        "text_rows": normal_values(key_of[0], (STREAM, D), 1.0, 6.0, ((0, 64), (1, 8))),
        "picture_rows": draw_picture_rows(jax.random.fold_in(key_of[12], 71), 0),
        "picture_slots": draw_picture_slots(jax.random.fold_in(key_of[12], 71), 0),
        "norm_gain": jnp.clip(1.0 + 0.18 * jax.random.normal(key_of[3], (D,), jnp.float32), 0.1, 1.9),
        "w_query": draw_w_query(jax.random.fold_in(key_of[12], 71), 0),
        "w_key": draw_w_key(jax.random.fold_in(key_of[12], 71), 0),
        "w_value": normal_values(key_of[6], (D, KV_HEADS * HD), D ** -0.5, 0.09375, ((0, 64), (1, 8))),
        "w_out": normal_values(key_of[7], (HEADS * HD, D), HD ** -0.5, 0.5, ((0, 8), (1, 64))),
        "cache_keys": draw_cache_keys(jax.random.fold_in(key_of[12], 71), 0),
        "cache_values": normal_values(key_of[9], (CACHE, KV_HEADS * HD), 1.0, 6.0, ((0, 64), (1, 8))),
        "recompute_rows": normal_values(key_of[10], (RECOMP, D), 1.0, 6.0, ((0, 64), (1, 8))),
        "recompute_slots": draw_recompute_slots(jax.random.fold_in(key_of[12], 71), 0),
    }


EPSILON = 1e-05
ROPE_BASE = 1000000.0

def rotate(values, positions):
    half = values.shape[-1] // 2
    freqs = ROPE_BASE ** (-jnp.arange(half, dtype=jnp.float32) / half)
    angles = positions[:, None] * freqs[None, :]
    cosine = jnp.cos(angles)[:, None, :]
    sine = jnp.sin(angles)[:, None, :]
    first = values[..., :half]
    second = values[..., half:]
    return jnp.concatenate([first * cosine - second * sine, second * cosine + first * sine], axis=-1)

def normalise(rows, gain):
    rows_wide = rows.astype(jnp.float32)
    squares = lax.optimization_barrier(jnp.sum(rows_wide * rows_wide, axis=1))
    return (rows_wide * lax.rsqrt(squares / D + EPSILON)[:, None] * gain[None, :]).astype(jnp.bfloat16)

def reference(text_rows, picture_rows, picture_slots, norm_gain, w_query, w_key, w_value, w_out, cache_keys, cache_values, recompute_rows, recompute_slots):
    stream = text_rows.at[picture_slots].set(picture_rows)
    normed = normalise(stream, norm_gain)
    rec_normed = normalise(recompute_rows, norm_gain)
    query = jnp.dot(normed, w_query, preferred_element_type=jnp.float32)
    key_new = jnp.dot(normed, w_key, preferred_element_type=jnp.float32)
    value_new = jnp.dot(normed, w_value, preferred_element_type=jnp.float32)
    rec_key = jnp.dot(rec_normed, w_key, preferred_element_type=jnp.float32)
    rec_value = jnp.dot(rec_normed, w_value, preferred_element_type=jnp.float32)
    stream_pos = (CACHE + jnp.arange(STREAM)).astype(jnp.float32)
    rec_pos = recompute_slots.astype(jnp.float32)
    rot_query = rotate(query.reshape(STREAM, HEADS, HD), stream_pos).astype(jnp.bfloat16).reshape(STREAM, HEADS * HD)
    rot_key = rotate(key_new.reshape(STREAM, KV_HEADS, HD), stream_pos).astype(jnp.bfloat16).reshape(STREAM, KV_HEADS * HD)
    rot_rec_key = rotate(rec_key.reshape(RECOMP, KV_HEADS, HD), rec_pos).astype(jnp.bfloat16).reshape(RECOMP, KV_HEADS * HD)
    all_keys = jnp.concatenate([cache_keys.at[recompute_slots].set(rot_rec_key), rot_key], axis=0)
    all_values = jnp.concatenate([cache_values.at[recompute_slots].set(rec_value.astype(jnp.bfloat16)), value_new.astype(jnp.bfloat16)], axis=0)
    rows_index = jnp.arange(STREAM, dtype=jnp.int32)
    cols_index = jnp.arange(CACHE + STREAM, dtype=jnp.int32)
    allowed = (cols_index[None, :] < CACHE) | (cols_index[None, :] - CACHE <= rows_index[:, None])
    group = HEADS // KV_HEADS

    def one_head(head_index):
        kv_index = head_index // group
        head_query = lax.dynamic_slice_in_dim(rot_query, head_index * HD, HD, 1)
        head_keys = lax.dynamic_slice_in_dim(all_keys, kv_index * HD, HD, 1)
        head_values = lax.dynamic_slice_in_dim(all_values, kv_index * HD, HD, 1)
        scores = jnp.dot(head_query, head_keys.T, preferred_element_type=jnp.float32) * HD ** (-0.5)
        scores = jnp.where(allowed, scores, -1e+30)
        top = lax.optimization_barrier(jnp.max(scores, axis=1, keepdims=True))
        weights = jnp.where(allowed, jnp.exp(scores - top), 0.0)
        total = lax.optimization_barrier(jnp.sum(weights, axis=1, keepdims=True))
        return jnp.dot(weights.astype(jnp.bfloat16), head_values, preferred_element_type=jnp.float32) / total
    heads_out = lax.map(one_head, jnp.arange(HEADS, dtype=jnp.int32))
    attended = jnp.transpose(heads_out, (1, 0, 2)).reshape(STREAM, HEADS * HD).astype(jnp.bfloat16)
    return jnp.dot(attended, w_out, preferred_element_type=jnp.float32).astype(jnp.bfloat16)
```

```python
import functools
import math

import jax
import jax.numpy as jnp
from jax import lax
from jax.experimental import pallas as pl
from jax.experimental.pallas import tpu as pltpu
from jax.sharding import PartitionSpec as P

D = 4096
HD = 128
NX, NY, NC, NZ = 4, 8, 2, 8
MESH = pl.DeviceIdType.MESH

EPSILON = 1e-05
ROPE_BASE = 1000000.0
NEG_FILL = -1e30


def rotate(values, positions):
    half = values.shape[-1] // 2
    freqs = ROPE_BASE ** (-jnp.arange(half, dtype=jnp.float32) / half)
    angles = positions[:, None] * freqs[None, :]
    cosine = jnp.cos(angles)[:, None, :]
    sine = jnp.sin(angles)[:, None, :]
    first = values[..., :half]
    second = values[..., half:]
    return jnp.concatenate(
        [first * cosine - second * sine, second * cosine + first * sine], axis=-1
    )


def place():
    s = lax.axis_index("seq")
    return s // (NY * NC), (s // NC) % NY, s % NC


def seq_of(x, y, c):
    return ((x % NX) * NY + y % NY) * NC + c


class Sends:
    def __init__(self, send_sems, recv_sems):
        self.send_sems, self.recv_sems, self.made = send_sems, recv_sems, []

    def start(self, src, dst, device_id):
        at = len(self.made)
        copy = pltpu.make_async_remote_copy(
            src_ref=src,
            dst_ref=dst,
            send_sem=self.send_sems.at[at],
            recv_sem=self.recv_sems.at[at],
            device_id=device_id,
            device_id_type=MESH,
        )
        copy.start()
        self.made.append(copy)
        return copy

    def finish(self):
        for copy in self.made:
            copy.wait_send()


def wait_all(copies):
    for copy in copies:
        copy.wait_recv()


PLANE_COPIES = 58
LINE_COPIES = 7


def plane_steps(src, out, sends, local_sem):
    x, y, c = place()
    half = src.shape[0] // 2
    a_rows, b_rows = pl.ds(0, half), pl.ds(half, half)
    every_x = pl.ds(0, NX)
    up = {"seq": seq_of(x, y + 1, c)}
    down = {"seq": seq_of(x, y + NY - 1, c)}
    right = {"seq": seq_of(x + 1, y, c)}
    left = {"seq": seq_of(x + NX - 1, y, c)}
    other = {"seq": seq_of(x, y, 1 - c)}

    def col(k):
        return (y + k + NY) % NY

    def a_block(xs, k):
        return out.at[xs, col(k), c, a_rows]

    def b_block(xx, k):
        return out.at[xx, col(k), c, b_rows]

    def spread(k):
        block = b_block(x, k)
        return [sends.start(block, block, right), sends.start(block, block, left)]

    def forward(k):
        odd = col(k) % 2
        block = b_block((x + NX - 1 + 2 * odd) % NX, k)
        return sends.start(block, block, {"seq": seq_of(x + 1 + 2 * odd, y, c)})

    def hand(ref):
        return sends.start(ref, ref, other)

    own = pltpu.make_async_copy(src, out.at[x, y, c], local_sem)
    own.start()
    along = [
        sends.start(src.at[a_rows], a_block(x, 0), {"seq": seq_of(x + d, y, c)}) for d in (1, 2, 3)
    ]
    own.wait()
    ring_b = [sends.start(b_block(x, 0), b_block(x, 0), to) for to in (up, down)]
    spreads = {0: spread(0)}
    forwards, handed = {}, []
    ring_a = []
    yield
    for k in range(1, NY // 2 + 3):
        if k == 1:
            wait_all(along)
        elif k <= NY // 2 + 1:
            wait_all(ring_a)
        if k <= NY // 2:
            if k < NY // 2:
                parts = (every_x, every_x)
            else:
                parts = (pl.ds(0, NX // 2), pl.ds(NX // 2, NX // 2))
            ring_a = [
                sends.start(a_block(parts[0], 1 - k), a_block(parts[0], 1 - k), up),
                sends.start(a_block(parts[1], k - 1), a_block(parts[1], k - 1), down),
            ]
        if k == 1:
            handed.append(hand(a_block(every_x, 0)))
        elif k <= NY // 2:
            handed.append(hand(a_block(every_x, 1 - k)))
            handed.append(hand(a_block(every_x, k - 1)))
        elif k == NY // 2 + 1:
            handed.append(hand(a_block(every_x, k - 1)))
        if k <= NY // 2:
            wait_all(ring_b)
            if k < NY // 2:
                ring_b = [sends.start(b_block(x, -k), b_block(x, -k), up)]
                if k < NY // 2 - 1:
                    ring_b.append(sends.start(b_block(x, k), b_block(x, k), down))
                for j in (-k, k):
                    spreads[j] = spread(j)
            else:
                spreads[-k] = spread(-k)
        arrived = k - 1
        if arrived <= NY // 2:
            for j in {0: (0,), NY // 2: (-NY // 2,)}.get(arrived, (-arrived, arrived)):
                wait_all(spreads[j])
                forwards[j] = forward(j)
        arrived = k - 2
        if arrived >= 0:
            for j in {0: (0,), NY // 2: (-NY // 2,)}.get(arrived, (-arrived, arrived)):
                wait_all([forwards[j]])
                handed.append(hand(b_block(every_x, j)))
        yield
    wait_all(handed)


def line_steps(src, out, sends, local_sem):
    z = lax.axis_index("head")
    up = {"head": (z + 1) % NZ}
    down = {"head": (z + NZ - 1) % NZ}

    def block(k):
        return out.at[(z + k + NZ) % NZ]

    own = pltpu.make_async_copy(src, block(0), local_sem)
    own.start()
    ring = [sends.start(src, block(0), to) for to in (up, down)]
    own.wait()
    yield
    for k in range(1, NZ // 2 + 1):
        wait_all(ring)
        ring = []
        if k < NZ // 2:
            ring.append(sends.start(block(-k), block(-k), up))
        if k < NZ // 2 - 1:
            ring.append(sends.start(block(k), block(k), down))
        yield


def greet(plane, line):
    x, y, c = place()
    z = lax.axis_index("head")
    partners = []
    if plane:
        partners += [{"seq": seq_of(x + d, y, c)} for d in (1, 2, 3)]
        partners += [{"seq": seq_of(x, y + d, c)} for d in (1, NY - 1)]
        partners += [{"seq": seq_of(x, y, 1 - c)}]
    partners += [{"head": (z + d) % NZ} for d in line]
    barrier = pltpu.get_barrier_semaphore()
    for partner in partners:
        pl.semaphore_signal(barrier, inc=1, device_id=partner, device_id_type=MESH)
    pl.semaphore_wait(barrier, len(partners))


def gather_kernel(planes, lines, *refs):
    total = planes + lines
    ins, outs = refs[:total], refs[total : 2 * total]
    send_sems, recv_sems, local_sems = refs[2 * total :]
    greet(planes > 0, (1, NZ - 1) if lines else ())
    sends = Sends(send_sems, recv_sems)
    runs = [plane_steps(ins[i], outs[i], sends, local_sems.at[i]) for i in range(planes)]
    runs += [line_steps(ins[i], outs[i], sends, local_sems.at[i]) for i in range(planes, total)]
    while runs:
        runs = [run for run in runs if next(run, runs) is not runs]
    sends.finish()


def gather(plane_arrays, line_arrays, collective_id):
    arrays = list(plane_arrays) + list(line_arrays)
    copies = PLANE_COPIES * len(plane_arrays) + LINE_COPIES * len(line_arrays)
    shapes = [(NX, NY, NC) + a.shape for a in plane_arrays] + [(NZ,) + a.shape for a in line_arrays]
    anywhere = pl.BlockSpec(memory_space=pl.ANY)
    return pl.pallas_call(
        functools.partial(gather_kernel, len(plane_arrays), len(line_arrays)),
        out_shape=[jax.ShapeDtypeStruct(shape, jnp.bfloat16) for shape in shapes],
        in_specs=[anywhere] * len(arrays),
        out_specs=[anywhere] * len(arrays),
        scratch_shapes=[
            pltpu.SemaphoreType.DMA((copies,)),
            pltpu.SemaphoreType.DMA((copies,)),
            pltpu.SemaphoreType.DMA((len(arrays),)),
        ],
        compiler_params=pltpu.CompilerParams(collective_id=collective_id, has_side_effects=True),
    )(*arrays)


def exchange_kernel(src, out, send_sems, recv_sems, local_sem):
    z = lax.axis_index("head")
    greet(False, range(1, NZ))
    own = pltpu.make_async_copy(src.at[z], out.at[0], local_sem)
    own.start()
    copies = []
    for d in range(1, NZ):
        copy = pltpu.make_async_remote_copy(
            src_ref=src.at[(z + d) % NZ],
            dst_ref=out.at[d],
            send_sem=send_sems.at[d],
            recv_sem=recv_sems.at[d],
            device_id={"head": (z + d) % NZ},
            device_id_type=MESH,
        )
        copy.start()
        copies.append(copy)
    own.wait()
    for copy in copies:
        copy.wait()


def exchange(blocks, collective_id):
    anywhere = pl.BlockSpec(memory_space=pl.ANY)
    return pl.pallas_call(
        exchange_kernel,
        out_shape=jax.ShapeDtypeStruct(blocks.shape, blocks.dtype),
        in_specs=[anywhere],
        out_specs=anywhere,
        scratch_shapes=[
            pltpu.SemaphoreType.DMA((NZ,)),
            pltpu.SemaphoreType.DMA((NZ,)),
            pltpu.SemaphoreType.DMA,
        ],
        compiler_params=pltpu.CompilerParams(collective_id=collective_id, has_side_effects=True),
    )(blocks)


def attend_kernel(tok, cache, group, q_ref, kv_ref, o_ref, best, total, accum):
    step = pl.program_id(0)
    s = lax.axis_index("seq")
    span = kv_ref.shape[0]
    rows = cache + tok
    scale = HD**-0.5 * math.log2(math.e)

    @pl.when(step == 0)
    def _():
        best[...] = jnp.full_like(best, NEG_FILL)
        total[...] = jnp.zeros_like(total)
        accum[...] = jnp.zeros_like(accum)

    def update(keys, values, mask):
        scores = lax.dot_general(
            q_ref[...], keys, (((1,), (1,)), ((), ())), preferred_element_type=jnp.float32
        )
        if mask is not None:
            scores = jnp.where(mask, scores, NEG_FILL)
        old = best[...]
        fresh = jnp.maximum(old, jnp.max(scores, axis=1, keepdims=True))
        factor = jnp.exp2((old - fresh) * scale)
        weights = jnp.exp2((scores - fresh) * scale)
        best[...] = fresh
        total[...] = total[...] * factor + jnp.sum(weights, axis=1, keepdims=True)
        accum[...] = accum[...] * factor + jnp.dot(
            weights.astype(jnp.bfloat16), values, preferred_element_type=jnp.float32
        )

    def whole():
        block = kv_ref[...]
        return (
            block[:, :, :HD].reshape(span * rows, HD),
            block[:, :, HD:].reshape(span * rows, HD),
        )

    @pl.when(step < s // span)
    def _():
        keys, values = whole()
        update(keys, values, None)

    @pl.when(step == s // span)
    def _():
        keys, values = whole()
        at = lax.broadcasted_iota(jnp.int32, (1, span * rows), 1)
        row = at % rows
        key_pos = jnp.where(row < cache, -1, (step * span + at // rows) * tok + row - cache)
        query_at = lax.broadcasted_iota(jnp.int32, (group * tok, 1), 0)
        query_pos = s * tok + query_at % tok
        update(keys, values, key_pos <= query_pos)

    @pl.when(step > s // span)
    def _():
        block = kv_ref[:, :cache, :]
        update(
            block[:, :, :HD].reshape(span * cache, HD),
            block[:, :, HD:].reshape(span * cache, HD),
            None,
        )

    @pl.when(step == pl.num_programs(0) - 1)
    def _():
        out = accum[...] / total[...]
        for g in range(group):
            o_ref[:, g * HD : (g + 1) * HD] = out[g * tok : (g + 1) * tok].astype(o_ref.dtype)


def attend(queries, kv, tok, cache, group):
    span = 8
    blocks, rows, width = kv.shape
    return pl.pallas_call(
        functools.partial(attend_kernel, tok, cache, group),
        out_shape=jax.ShapeDtypeStruct((tok, group * HD), jnp.bfloat16),
        grid=(blocks // span,),
        in_specs=[
            pl.BlockSpec((group * tok, HD), lambda i: (0, 0)),
            pl.BlockSpec((span, rows, width), lambda i: (i, 0, 0)),
        ],
        out_specs=pl.BlockSpec((tok, group * HD), lambda i: (0, 0)),
        scratch_shapes=[
            pltpu.VMEM((group * tok, 1), jnp.float32),
            pltpu.VMEM((group * tok, 1), jnp.float32),
            pltpu.VMEM((group * tok, HD), jnp.float32),
        ],
        compiler_params=pltpu.CompilerParams(vmem_limit_bytes=40 * 1024 * 1024),
    )(queries, kv)


def on_device(
    text_rows,
    picture_rows,
    picture_slots,
    norm_gain,
    w_query,
    w_key,
    w_value,
    w_out,
    cache_keys,
    cache_values,
    recompute_rows,
    recompute_slots,
):
    tok_rows, slice_width = text_rows.shape
    rec_count = recompute_rows.shape[0]
    cache_rows = cache_keys.shape[0]
    query_cols = w_query.shape[1]
    key_cols = w_key.shape[1]
    group = query_cols // HD
    seq_index = lax.axis_index("seq")
    local_pos = seq_index * tok_rows + jnp.arange(tok_rows, dtype=jnp.int32)
    digits = jnp.stack([picture_slots // HD, picture_slots % HD], axis=1).astype(jnp.bfloat16)
    digits = jnp.pad(digits, ((0, 0), (0, HD - 2)))
    (pictures,) = gather([jnp.concatenate([picture_rows, digits], axis=1)], [], 0)
    pictures = pictures.reshape(-1, slice_width + HD)
    digits = pictures[:, slice_width : slice_width + 2].astype(jnp.int32)
    slots = digits[:, 0] * HD + digits[:, 1]
    select = (slots[None, :] == local_pos[:, None]).astype(jnp.bfloat16)
    placed = jnp.dot(select, pictures[:, :slice_width], preferred_element_type=jnp.float32)
    hits = jnp.sum(select.astype(jnp.float32), axis=1)
    stream = jnp.where(hits[:, None] > 0.5, placed, text_rows.astype(jnp.float32)).astype(
        jnp.bfloat16
    )
    raw = jnp.concatenate([stream, recompute_rows], axis=0)
    weights = jnp.concatenate([w_query, w_key, w_value, w_out.T], axis=1)
    weights, raw = gather([weights], [raw], 1)
    weights = weights.reshape(D, -1)
    raw = jnp.transpose(raw, (1, 0, 2)).reshape(tok_rows + rec_count, D)
    wide = raw.astype(jnp.float32)
    squares = jnp.sum(wide * wide, axis=1)
    normed = (wide * lax.rsqrt(squares / D + EPSILON)[:, None] * norm_gain[None, :]).astype(
        jnp.bfloat16
    )
    in_cols = query_cols + 2 * key_cols
    projected = jnp.dot(normed, weights[:, :in_cols], preferred_element_type=jnp.float32)
    heads = projected[:, : query_cols + key_cols].reshape(-1, group + 1, HD)
    cache_total = cache_rows * lax.axis_size("seq")
    positions = jnp.concatenate([cache_total + local_pos, recompute_slots]).astype(jnp.float32)
    rotated = rotate(heads, positions).astype(jnp.bfloat16)
    values = projected[:, query_cols + key_cols :].astype(jnp.bfloat16)
    kv = jnp.concatenate([rotated[:, group], values], axis=1)
    local_slots = recompute_slots - seq_index * cache_rows
    select = local_slots[:, None] == jnp.arange(cache_rows, dtype=jnp.int32)[None, :]
    replaced = jnp.any(select, axis=0)[:, None]
    fresh = jnp.dot(
        select.astype(jnp.bfloat16).T, kv[tok_rows:], preferred_element_type=jnp.float32
    ).astype(jnp.bfloat16)
    cache = jnp.where(replaced, fresh, jnp.concatenate([cache_keys, cache_values], axis=1))
    (kv_all,) = gather([jnp.concatenate([cache, kv[:tok_rows]], axis=0)], [], 2)
    queries = jnp.transpose(rotated[:tok_rows, :group], (1, 0, 2)).reshape(group * tok_rows, HD)
    attended = attend(
        queries,
        kv_all.reshape(-1, cache_rows + tok_rows, 2 * HD),
        tok_rows,
        cache_rows,
        group,
    )
    partial_out = lax.dot_general(
        weights[:, in_cols:].reshape(NZ, slice_width, query_cols),
        attended,
        (((2,), (1,)), ((), ())),
        preferred_element_type=jnp.float32,
    ).astype(jnp.bfloat16)
    parts = exchange(jnp.transpose(partial_out, (0, 2, 1)), 3)
    return jnp.sum(parts.astype(jnp.float32), axis=0).astype(jnp.bfloat16)


def solution(mesh):
    return jax.shard_map(
        on_device,
        mesh=mesh,
        in_specs=(
            P("seq", "head"),
            P("seq", "head"),
            P("seq"),
            P(),
            P("seq", "head"),
            P("seq", "head"),
            P("seq", "head"),
            P("head", "seq"),
            P("seq", "head"),
            P("seq", "head"),
            P("seq", "head"),
            P("seq"),
        ),
        out_specs=P("seq", "head"),
        check_vma=False,
    )
```

```python
import functools
import math

import jax
import jax.numpy as jnp
from jax import lax
from jax.experimental import pallas as pl
from jax.experimental.pallas import tpu as pltpu
from jax.sharding import PartitionSpec as P

D = 4096
HD = 128
NX, NY, NC, NZ = 4, 8, 2, 8
MESH = pl.DeviceIdType.MESH

EPSILON = 1e-05
ROPE_BASE = 1000000.0
NEG_FILL = -1e30


def place():
    s = lax.axis_index("seq")
    return s // (NY * NC), (s // NC) % NY, s % NC


def seq_of(x, y, c):
    return ((x % NX) * NY + y % NY) * NC + c


class Sends:
    def __init__(self, send_sems, recv_sems):
        self.send_sems, self.recv_sems, self.made = send_sems, recv_sems, []

    def start(self, src, dst, device_id):
        at = len(self.made)
        copy = pltpu.make_async_remote_copy(
            src_ref=src,
            dst_ref=dst,
            send_sem=self.send_sems.at[at],
            recv_sem=self.recv_sems.at[at],
            device_id=device_id,
            device_id_type=MESH,
        )
        copy.start()
        self.made.append(copy)
        return copy

    def finish(self):
        for copy in self.made:
            copy.wait_send()


def wait_all(copies):
    for copy in copies:
        copy.wait_recv()


def ring_near(n, block, source, to, sends):
    return [sends.start(source, block(0), to(d)) for d in (2, -2, 1, -1)]


def ring_far(at, block, to, sends):
    odd = at % 2
    return [
        sends.start(block(-2), block(-2), to(1)),
        sends.start(block(2), block(2), to(-1)),
        sends.start(block(4 * odd - 2), block(4 * odd - 2), to(2 - 4 * odd)),
    ]


NEAR = (-2, 2, -1, 1)
FAR = (-3, 3, 4)


def plane_steps(src, out, sends, local_sem, split):
    x, y, c = place()
    a_rows, b_rows = pl.ds(0, split), pl.ds(split, src.shape[0] - split)
    every_x = pl.ds(0, NX)
    right = {"seq": seq_of(x + 1, y, c)}
    left = {"seq": seq_of(x + NX - 1, y, c)}
    other = {"seq": seq_of(x, y, 1 - c)}

    def col(k):
        return (y + k + NY) % NY

    def up(k):
        return {"seq": seq_of(x, y + k + NY, c)}

    def a_block(k):
        return out.at[every_x, col(k), c, a_rows]

    def b_block(k, xx=x):
        return out.at[xx, col(k), c, b_rows]

    def spread(k, source=None):
        source = b_block(k) if source is None else source
        return [sends.start(source, b_block(k), right), sends.start(source, b_block(k), left)]

    def forward(k):
        odd = col(k) % 2
        block = b_block(k, (x + NX - 1 + 2 * odd) % NX)
        return sends.start(block, block, {"seq": seq_of(x + 1 + 2 * odd, y, c)})

    handed = []

    def hand(ref):
        handed.append(sends.start(ref, ref, other))

    own = pltpu.make_async_copy(src, out.at[x, y, c], local_sem)
    own.start()
    ring_b = ring_near(NY, b_block, src.at[b_rows], up, sends)
    if split:
        along = [
            sends.start(src.at[a_rows], out.at[x, y, c, a_rows], {"seq": seq_of(x + d, y, c)})
            for d in (2, 1, 3)
        ]
    own_spread = spread(0, src.at[b_rows])
    yield
    own.wait()
    if split:
        wait_all(along)
        ring_a = ring_near(NY, a_block, a_block(0), up, sends)
    wait_all(ring_b)
    ring_b = ring_far(y, b_block, up, sends)
    near_spread = [spread(k) for k in NEAR]
    if split:
        hand(a_block(0))
    wait_all(own_spread)
    own_forward = forward(0)
    yield
    if split:
        wait_all(ring_a)
        ring_a = ring_far(y, a_block, up, sends)
    wait_all(ring_b)
    far_spread = [spread(k) for k in FAR]
    near_forward = []
    for k, copies in zip(NEAR, near_spread):
        wait_all(copies)
        near_forward.append(forward(k))
    if split:
        for k in NEAR:
            hand(a_block(k))
    wait_all([own_forward])
    hand(b_block(0, every_x))
    yield
    far_forward = []
    for k, copies in zip(FAR, far_spread):
        wait_all(copies)
        far_forward.append(forward(k))
    if split:
        wait_all(ring_a)
        for k in FAR:
            hand(a_block(k))
    for k, copy in zip(NEAR, near_forward):
        wait_all([copy])
        hand(b_block(k, every_x))
    yield
    for k, copy in zip(FAR, far_forward):
        wait_all([copy])
        hand(b_block(k, every_x))
    yield
    wait_all(handed)


def line_steps(src, out, sends, local_sem):
    z = lax.axis_index("head")

    def to(k):
        return {"head": (z + k + NZ) % NZ}

    def block(k):
        return out.at[(z + k + NZ) % NZ]

    own = pltpu.make_async_copy(src, block(0), local_sem)
    own.start()
    ring = ring_near(NZ, block, src, to, sends)
    own.wait()
    yield
    wait_all(ring)
    ring = ring_far(z, block, to, sends)
    yield
    wait_all(ring)


def greet():
    x, y, c = place()
    z = lax.axis_index("head")
    partners = [{"seq": seq_of(x + d, y, c)} for d in (1, 2, 3)]
    partners += [{"seq": seq_of(x, y + d, c)} for d in (1, 2, NY - 2, NY - 1)]
    partners += [{"seq": seq_of(x, y, 1 - c)}]
    partners += [{"head": (z + d) % NZ} for d in range(1, NZ)]
    barrier = pltpu.get_barrier_semaphore()
    for partner in partners:
        pl.semaphore_signal(barrier, inc=1, device_id=partner, device_id_type=MESH)
    pl.semaphore_wait(barrier, len(partners))


PIC_COPIES = 39
PLANE_COPIES = 57
LINE_COPIES = 7


def advance(*runs):
    for run in runs:
        next(run, None)


def block_kernel(
    dims,
    pics,
    text,
    rec,
    w_in,
    w_out,
    gain,
    cosine,
    sine,
    cache,
    chosen,
    out,
    pics_all,
    raw,
    raw_all,
    w_in_all,
    w_out_all,
    kv_own,
    kv_all,
    queries,
    best,
    total,
    accum,
    attended,
    parts,
    arrived,
    send_sems,
    recv_sems,
    local_sems,
):
    tok, width, rec_count, cache_rows, group = dims
    s = lax.axis_index("seq")
    z = lax.axis_index("head")
    greet()
    sends = Sends(send_sems, recv_sems)
    pic_run = plane_steps(pics, pics_all, sends, local_sems.at[0], 0)
    in_run = plane_steps(w_in, w_in_all, sends, local_sems.at[1], 16)
    out_run = plane_steps(w_out, w_out_all, sends, local_sems.at[2], 16)
    advance(pic_run, pic_run, in_run, pic_run, pic_run, in_run, pic_run, out_run, pic_run)

    pictures = pics_all[...].reshape(-1, pics.shape[1])
    slot = pictures[:, width : width + 1].astype(jnp.float32) * HD + pictures[
        :, width + 1 : width + 2
    ].astype(jnp.float32)
    position = (s * tok + lax.broadcasted_iota(jnp.int32, (1, tok), 1)).astype(jnp.float32)
    select = (slot == position).astype(jnp.float32).astype(jnp.bfloat16)
    placed = lax.dot_general(
        select, pictures, (((0,), (0,)), ((), ())), preferred_element_type=jnp.float32
    )
    hit = placed[:, width + 2 : width + 3] > 0.5
    raw[:tok, :] = jnp.where(hit, placed[:, :width], text[...].astype(jnp.float32)).astype(
        jnp.bfloat16
    )
    raw[tok:, :] = rec[...]
    line_run = line_steps(raw, raw_all, sends, local_sems.at[3])
    advance(line_run, in_run, out_run, line_run, in_run, out_run, in_run, line_run)

    rows = raw.shape[0]
    squares = jnp.zeros((rows, 1), jnp.float32)
    for zz in range(NZ):
        wide = raw_all[zz].astype(jnp.float32)
        squares = squares + jnp.sum(wide * wide, axis=1, keepdims=True)
    shrink = lax.rsqrt(squares / D + EPSILON)
    advance(in_run, out_run)
    projected = jnp.zeros((rows, w_in.shape[1]), jnp.float32)
    half = NY // 2
    for zz in range(NZ):
        normed = (
            raw_all[zz].astype(jnp.float32) * shrink * gain[:, zz * width : (zz + 1) * width]
        ).astype(jnp.bfloat16)
        block = w_in_all[zz // 2, half * (zz % 2) : half * (zz % 2 + 1)].reshape(width, -1)
        projected = projected + jnp.dot(normed, block, preferred_element_type=jnp.float32)

    def rotated(at):
        values = projected[:, at * HD : (at + 1) * HD]
        return values * cosine[...] + pltpu.roll(values, HD // 2, 1) * sine[...]

    for g in range(group):
        queries[g * tok : (g + 1) * tok, :] = rotated(g)[:tok].astype(jnp.bfloat16)
    pair = jnp.concatenate([rotated(group), projected[:, (group + 1) * HD :]], axis=1)
    kv_own[cache_rows:, :] = pair[:tok].astype(jnp.bfloat16)
    fresh = pair[tok:].astype(jnp.bfloat16).astype(jnp.float32)
    kept = cache[...].astype(jnp.float32)
    for r in range(rec_count):
        kept = jnp.where(chosen[:, r : r + 1] > 0.5, fresh[r : r + 1, :], kept)
    kv_own[:cache_rows, :] = kept.astype(jnp.bfloat16)
    kv_run = plane_steps(kv_own, kv_all, sends, local_sems.at[4], 48)
    advance(kv_run, out_run, kv_run, out_run, kv_run, kv_run, kv_run, kv_run)

    best[...] = jnp.full_like(best, NEG_FILL)
    total[...] = jnp.zeros_like(total)
    accum[...] = jnp.zeros_like(accum)
    scale = HD**-0.5 * math.log2(math.e)
    kv_rows = cache_rows + tok
    span = half * NC

    def update(block, mask):
        keys, values = block[:, :HD], block[:, HD:]
        scores = lax.dot_general(
            queries[...], keys, (((1,), (1,)), ((), ())), preferred_element_type=jnp.float32
        )
        if mask is not None:
            scores = jnp.where(mask, scores, NEG_FILL)
        old = best[...]
        top = jnp.maximum(old, jnp.max(scores, axis=1, keepdims=True))
        factor = jnp.exp2((old - top) * scale)
        weights = jnp.exp2((scores - top) * scale)
        best[...] = top
        total[...] = total[...] * factor + jnp.sum(weights, axis=1, keepdims=True)
        accum[...] = accum[...] * factor + jnp.dot(
            weights.astype(jnp.bfloat16), values, preferred_element_type=jnp.float32
        )

    def visit(step, carry):
        xx, y0 = step // 2, half * (step % 2)

        @pl.when(step < s // span)
        def _():
            update(kv_all[xx, pl.ds(y0, half)].reshape(span * kv_rows, 2 * HD), None)

        @pl.when(step == s // span)
        def _():
            at = lax.broadcasted_iota(jnp.int32, (1, span * kv_rows), 1)
            row = at % kv_rows
            key_pos = jnp.where(
                row < cache_rows, -1, (step * span + at // kv_rows) * tok + row - cache_rows
            )
            query_pos = s * tok + lax.broadcasted_iota(jnp.int32, (group * tok, 1), 0) % tok
            update(
                kv_all[xx, pl.ds(y0, half)].reshape(span * kv_rows, 2 * HD), key_pos <= query_pos
            )

        @pl.when(step > s // span)
        def _():
            update(
                kv_all[xx, pl.ds(y0, half), :, pl.ds(0, cache_rows), :].reshape(
                    span * cache_rows, 2 * HD
                ),
                None,
            )

        return carry

    lax.fori_loop(0, NX * 2, visit, 0)
    result = accum[...] / total[...]
    for g in range(group):
        attended[:, g * HD : (g + 1) * HD] = result[g * tok : (g + 1) * tok].astype(jnp.bfloat16)
    advance(out_run)

    def columns(d):
        zz = (z + d) % NZ
        block = w_out_all[zz // 2, pl.ds(half * (zz % 2), half)].reshape(width, -1)
        return lax.dot_general(
            attended[...], block, (((1,), (1,)), ((), ())), preferred_element_type=jnp.float32
        )

    shares = []
    for d in (4, 3, 5, 2, 6, 1, 7):
        parts[d] = columns(d).astype(jnp.bfloat16)
        shares.append(sends.start(parts.at[d], arrived.at[d], {"head": (z + d) % NZ}))
    mixed = columns(0)
    wait_all(shares)
    for d in range(1, NZ):
        mixed = mixed + arrived[d].astype(jnp.float32)
    out[...] = mixed.astype(jnp.bfloat16)
    sends.finish()


def on_device(
    text_rows,
    picture_rows,
    picture_slots,
    norm_gain,
    w_query,
    w_key,
    w_value,
    w_out,
    cache_keys,
    cache_values,
    recompute_rows,
    recompute_slots,
):
    tok, width = text_rows.shape
    rec_count = recompute_rows.shape[0]
    cache_rows = cache_keys.shape[0]
    group = w_query.shape[1] // HD
    rec_rows = 16
    seq_index = lax.axis_index("seq")
    marks = jnp.stack(
        [picture_slots // HD, picture_slots % HD, jnp.ones_like(picture_slots)], axis=1
    ).astype(jnp.bfloat16)
    pics = jnp.concatenate([picture_rows, jnp.pad(marks, ((0, 0), (0, HD - 3)))], axis=1)
    rec = jnp.pad(recompute_rows, ((0, rec_rows - rec_count), (0, 0)))
    w_in = jnp.concatenate([w_query, w_key, w_value], axis=1)
    cache = jnp.concatenate([cache_keys, cache_values], axis=1)
    chosen = (
        (recompute_slots - seq_index * cache_rows)[None, :]
        == jnp.arange(cache_rows, dtype=jnp.int32)[:, None]
    ).astype(jnp.float32)
    positions = jnp.concatenate(
        [
            cache_rows * lax.axis_size("seq") + seq_index * tok + jnp.arange(tok, dtype=jnp.int32),
            jnp.pad(recompute_slots, (0, rec_rows - rec_count)),
        ]
    ).astype(jnp.float32)
    freqs = ROPE_BASE ** (-jnp.arange(HD // 2, dtype=jnp.float32) / (HD // 2))
    angles = positions[:, None] * freqs[None, :]
    cosine, sine = jnp.cos(angles), jnp.sin(angles)
    rows = tok + rec_rows
    kv_rows = cache_rows + tok
    plane = (NX, NY, NC)
    bf16, f32 = jnp.bfloat16, jnp.float32
    copies = PIC_COPIES + 3 * PLANE_COPIES + 2 * LINE_COPIES
    vmem = pl.BlockSpec(memory_space=pltpu.VMEM)
    operands = (
        pics,
        text_rows,
        rec,
        w_in,
        w_out.T,
        norm_gain[None, :],
        jnp.concatenate([cosine, cosine], axis=1),
        jnp.concatenate([-sine, sine], axis=1),
        cache,
        chosen,
    )
    return pl.pallas_call(
        functools.partial(block_kernel, (tok, width, rec_count, cache_rows, group)),
        out_shape=jax.ShapeDtypeStruct((tok, width), bf16),
        in_specs=[vmem] * len(operands),
        out_specs=vmem,
        scratch_shapes=[
            pltpu.VMEM(plane + pics.shape, bf16),
            pltpu.VMEM((rows, width), bf16),
            pltpu.VMEM((NZ, rows, width), bf16),
            pltpu.VMEM(plane + w_in.shape, bf16),
            pltpu.VMEM(plane + w_out.shape[::-1], bf16),
            pltpu.VMEM((kv_rows, 2 * HD), bf16),
            pltpu.VMEM(plane + (kv_rows, 2 * HD), bf16),
            pltpu.VMEM((group * tok, HD), bf16),
            pltpu.VMEM((group * tok, 1), f32),
            pltpu.VMEM((group * tok, 1), f32),
            pltpu.VMEM((group * tok, HD), f32),
            pltpu.VMEM((tok, group * HD), bf16),
            pltpu.VMEM((NZ, tok, width), bf16),
            pltpu.VMEM((NZ, tok, width), bf16),
            pltpu.SemaphoreType.DMA((copies,)),
            pltpu.SemaphoreType.DMA((copies,)),
            pltpu.SemaphoreType.DMA((5,)),
        ],
        compiler_params=pltpu.CompilerParams(
            collective_id=0, has_side_effects=True, vmem_limit_bytes=56 * 1024 * 1024
        ),
    )(*operands)


def solution(mesh):
    return jax.shard_map(
        on_device,
        mesh=mesh,
        in_specs=(
            P("seq", "head"),
            P("seq", "head"),
            P("seq"),
            P(),
            P("seq", "head"),
            P("seq", "head"),
            P("seq", "head"),
            P("head", "seq"),
            P("seq", "head"),
            P("seq", "head"),
            P("seq", "head"),
            P("seq"),
        ),
        out_specs=P("seq", "head"),
        check_vma=False,
    )
```

```python
import functools
import math

import jax
import jax.numpy as jnp
import numpy as np
from jax import lax
from jax.experimental import pallas as pl
from jax.experimental.pallas import tpu as pltpu
from jax.sharding import PartitionSpec as P

D = 4096
HD = 128
NX, NY, NC, NZ = 4, 8, 2, 8
MESH = pl.DeviceIdType.MESH

EPSILON = 1e-05
ROPE_BASE = 1000000.0
NEG_FILL = -1e30
ABSENT = 2.0**127


def place():
    s = lax.axis_index("seq")
    return s // (NY * NC), (s // NC) % NY, s % NC


def seq_of(x, y, c):
    return ((x % NX) * NY + y % NY) * NC + c


class Sends:
    def __init__(self, send_sems, recv_sems):
        self.send_sems, self.recv_sems, self.made = send_sems, recv_sems, []

    def start(self, src, dst, device_id):
        at = len(self.made)
        copy = pltpu.make_async_remote_copy(
            src_ref=src,
            dst_ref=dst,
            send_sem=self.send_sems.at[at],
            recv_sem=self.recv_sems.at[at],
            device_id=device_id,
            device_id_type=MESH,
        )
        copy.start()
        self.made.append(copy)
        return copy

    def finish(self):
        for copy in self.made:
            copy.wait_send()


def wait_all(copies):
    for copy in copies:
        copy.wait_recv()


def ring_near(n, block, source, to, sends):
    return [sends.start(source, block(0), to(d)) for d in (2, -2, 1, -1)]


def ring_far(at, block, to, sends):
    odd = at % 2
    return [
        sends.start(block(-2), block(-2), to(1)),
        sends.start(block(2), block(2), to(-1)),
        sends.start(block(4 * odd - 2), block(4 * odd - 2), to(2 - 4 * odd)),
    ]


NEAR = (-2, 2, -1, 1)
FAR = (-3, 3, 4)


def plane_steps(src, out, sends, local_sem, split):
    x, y, c = place()
    a_rows, b_rows = pl.ds(0, split), pl.ds(split, src.shape[0] - split)
    every_x = pl.ds(0, NX)
    right = {"seq": seq_of(x + 1, y, c)}
    left = {"seq": seq_of(x + NX - 1, y, c)}
    other = {"seq": seq_of(x, y, 1 - c)}

    def col(k):
        return (y + k + NY) % NY

    def up(k):
        return {"seq": seq_of(x, y + k + NY, c)}

    def a_block(k):
        return out.at[every_x, col(k), c, a_rows]

    def b_block(k, xx=x):
        return out.at[xx, col(k), c, b_rows]

    def spread(k, source=None):
        source = b_block(k) if source is None else source
        return [sends.start(source, b_block(k), right), sends.start(source, b_block(k), left)]

    def forward(k):
        odd = col(k) % 2
        block = b_block(k, (x + NX - 1 + 2 * odd) % NX)
        return sends.start(block, block, {"seq": seq_of(x + 1 + 2 * odd, y, c)})

    handed = []

    def hand(ref):
        handed.append(sends.start(ref, ref, other))

    own = pltpu.make_async_copy(src, out.at[x, y, c], local_sem)
    own.start()
    ring_b = ring_near(NY, b_block, src.at[b_rows], up, sends)
    if split:
        along = [
            sends.start(src.at[a_rows], out.at[x, y, c, a_rows], {"seq": seq_of(x + d, y, c)})
            for d in (2, 1, 3)
        ]
    own_spread = spread(0, src.at[b_rows])
    yield
    own.wait()
    if split:
        wait_all(along)
        ring_a = ring_near(NY, a_block, a_block(0), up, sends)
    wait_all(ring_b)
    ring_b = ring_far(y, b_block, up, sends)
    near_spread = [spread(k) for k in NEAR]
    if split:
        hand(a_block(0))
    wait_all(own_spread)
    own_forward = forward(0)
    yield
    if split:
        wait_all(ring_a)
        ring_a = ring_far(y, a_block, up, sends)
    wait_all(ring_b)
    far_spread = [spread(k) for k in FAR]
    near_forward = []
    for k, copies in zip(NEAR, near_spread):
        wait_all(copies)
        near_forward.append(forward(k))
    if split:
        for k in NEAR:
            hand(a_block(k))
    wait_all([own_forward])
    hand(b_block(0, every_x))
    yield
    far_forward = []
    for k, copies in zip(FAR, far_spread):
        wait_all(copies)
        far_forward.append(forward(k))
    if split:
        wait_all(ring_a)
        for k in FAR:
            hand(a_block(k))
    for k, copy in zip(NEAR, near_forward):
        wait_all([copy])
        hand(b_block(k, every_x))
    yield
    for k, copy in zip(FAR, far_forward):
        wait_all([copy])
        hand(b_block(k, every_x))
    yield
    wait_all(handed)


def line_steps(src, out, sends, local_sem, seen):
    z = lax.axis_index("head")
    odd = z % 2
    up, down = {"head": (z + 1) % NZ}, {"head": (z + NZ - 1) % NZ}

    def block(k):
        return out.at[(z + k + NZ) % NZ]

    own = pltpu.make_async_copy(src, block(0), local_sem)
    own.start()
    ring = [sends.start(src, block(0), up), sends.start(src, block(0), down)]
    own.wait()
    seen(z)
    yield
    for k in range(1, NZ // 2):
        wait_all(ring)
        if k < NZ // 2 - 1:
            ring = [
                sends.start(block(-k), block(-k), up),
                sends.start(block(k), block(k), down),
            ]
        else:
            far = block(k * (2 * odd - 1))
            ring = [sends.start(far, far, {"head": (z + 1 + odd * (NZ - 2)) % NZ})]
        seen((z - k + NZ) % NZ)
        seen((z + k) % NZ)
        yield
    wait_all(ring)
    seen((z + NZ // 2) % NZ)


def greet():
    x, y, c = place()
    z = lax.axis_index("head")
    partners = [{"seq": seq_of(x + d, y, c)} for d in (1, 2, 3)]
    partners += [{"seq": seq_of(x, y + d, c)} for d in (1, 2, NY - 2, NY - 1)]
    partners += [{"seq": seq_of(x, y, 1 - c)}]
    partners += [{"head": (z + d) % NZ} for d in range(1, NZ)]
    barrier = pltpu.get_barrier_semaphore()
    for partner in partners:
        pl.semaphore_signal(barrier, inc=1, device_id=partner, device_id_type=MESH)
    pl.semaphore_wait(barrier, len(partners))


START = "p"
PLACING = "pipipcpip"
LINING = "iclo" "ilci" "locl"
NORMING = "co"
KEYING = ("c", "ko", "ko", "ko", "kko")

PIC_COPIES = 39
PLANE_COPIES = 57
LINE_COPIES = 7


def advance(*runs):
    for run in runs:
        next(run, None)


def drain(run):
    for _ in run:
        pass


def block_kernel(dims, *refs):
    tok, width, rec_count, cache_rows, group = dims
    operands, refs = refs[:13], refs[13:]
    hbm_in = operands[:9]
    gain, freqs, slots, rec_slots = operands[9:]
    out, refs = refs[0], refs[1:]
    pics, text, rec, w_in, w_out, cache = refs[:6]
    turns, cache_own, raw, kv_own = refs[6:10]
    pics_all, raw_all, w_in_all, w_out_all, cache_all, kv_all = refs[10:16]
    squares, queries, best, accum, attended = refs[16:21]
    parts, sums, relayed, arrived = refs[21:25]
    send_sems, recv_sems, local_sems, load_sems = refs[25:]

    s = lax.axis_index("seq")
    z = lax.axis_index("head")
    key_cols = HD
    query_cols = group * HD
    places = (
        pics.at[:, pl.ds(0, width)],
        text,
        rec,
        w_in.at[:, pl.ds(0, query_cols)],
        w_in.at[:, pl.ds(query_cols, key_cols)],
        w_in.at[:, pl.ds(query_cols + key_cols, key_cols)],
        w_out,
        cache.at[:, pl.ds(0, key_cols)],
        cache.at[:, pl.ds(key_cols, key_cols)],
    )
    loads = [
        pltpu.make_async_copy(given, here, load_sems.at[i])
        for i, (given, here) in enumerate(zip(hbm_in, places))
    ]
    for load in loads:
        load.start()

    def column(values, count):
        shape = (count, values.shape[1])
        row = lax.broadcasted_iota(jnp.int32, shape, 0)
        lane = lax.broadcasted_iota(jnp.int32, shape, 1)
        return jnp.sum(jnp.where(row == lane, values, 0), axis=1, keepdims=True)

    at_stream = column(slots[...], pics.shape[0])
    lane = lax.broadcasted_iota(jnp.int32, (pics.shape[0], HD), 1)
    marks = jnp.where(lane == 0, at_stream // HD, jnp.where(lane == 1, at_stream % HD, 1))
    pics[:, width:] = marks.astype(jnp.float32).astype(jnp.bfloat16)
    greet()
    for load in loads:
        load.wait()
    sends = Sends(send_sems, recv_sems)
    pic_run = plane_steps(pics, pics_all, sends, local_sems.at[0], 0)
    in_run = plane_steps(w_in, w_in_all, sends, local_sems.at[1], 16)
    out_run = plane_steps(w_out, w_out_all, sends, local_sems.at[2], 16)
    cache_run = plane_steps(cache_own, cache_all, sends, local_sems.at[3], 16)
    runs = {"p": pic_run, "i": in_run, "o": out_run, "c": cache_run}

    def go(order):
        for name in order:
            advance(*(runs[name] if name == "l" else [runs[name]]))

    go(START)

    cache_at = lax.broadcasted_iota(jnp.int32, (cache_rows, rec_count), 0) + s * cache_rows
    chosen = (cache_at == rec_slots[...]).astype(jnp.float32)
    gone = jnp.max(chosen, axis=1, keepdims=True) > 0.5
    kept_keys = cache[:, :HD].astype(jnp.float32)
    repeat = kept_keys[rec_count : rec_count + 1]
    for r in range(rec_count - 1, -1, -1):
        repeat = jnp.where(gone[r : r + 1], repeat, kept_keys[r : r + 1])
    cache_own[:, :HD] = jnp.where(gone, repeat, kept_keys).astype(jnp.bfloat16)
    cache_own[:, HD:] = jnp.where(gone, ABSENT, cache[:, HD:].astype(jnp.float32)).astype(
        jnp.bfloat16
    )

    rows = raw.shape[1]
    lane = lax.broadcasted_iota(jnp.int32, (1, HD), 1)
    stream_at = lax.broadcasted_iota(jnp.int32, (tok, 1), 0) + (s * tok + NX * NY * NC * cache_rows)
    for first, place_of in ((0, stream_at), (tok, column(rec_slots[...], rows - tok))):
        angles = place_of.astype(jnp.float32) * freqs[...]
        sine = jnp.sin(angles)
        last = first + angles.shape[0]
        turns[first:last, :HD] = jnp.cos(angles)
        turns[first:last, HD:] = jnp.where(lane < HD // 2, -sine, sine)
    go(PLACING)
    drain(pic_run)

    pictures = pics_all[...].reshape(-1, pics.shape[1])
    slot = pictures[:, width : width + 1].astype(jnp.float32) * HD + pictures[
        :, width + 1 : width + 2
    ].astype(jnp.float32)
    position = (s * tok + lax.broadcasted_iota(jnp.int32, (1, tok), 1)).astype(jnp.float32)
    select = (slot == position).astype(jnp.float32).astype(jnp.bfloat16)
    placed = lax.dot_general(
        select, pictures, (((0,), (0,)), ((), ())), preferred_element_type=jnp.float32
    )
    hit = placed[:, width + 2 : width + 3] > 0.5
    stream = jnp.where(hit, placed[:, :width], text[...].astype(jnp.float32)).astype(jnp.bfloat16)
    part = width // 2
    extra = jnp.concatenate(
        [
            rec[...].astype(jnp.float32),
            jnp.zeros((rows - tok - rec_count, width), jnp.float32),
        ],
        axis=0,
    ).astype(jnp.bfloat16)
    squares[...] = jnp.zeros_like(squares)

    def line(j):
        def seen(at):
            wide = raw_all[j, at].astype(jnp.float32)
            squares[...] += jnp.sum(wide * wide, axis=1, keepdims=True)

        return line_steps(raw.at[j], raw_all.at[j], sends, local_sems.at[4 + j], seen)

    lines = [line(j) for j in range(2)]
    runs["l"] = lines
    for j in range(2):
        raw[j, :tok, :] = stream[:, j * part : (j + 1) * part]
        raw[j, tok:, :] = extra[:, j * part : (j + 1) * part]
        advance(lines[j])
    go(LINING)
    drain(lines[0])
    drain(lines[1])

    shrink = lax.rsqrt(squares[...] / D + EPSILON)
    go(NORMING)
    drain(in_run)
    projected = jnp.zeros((rows, w_in.shape[1]), jnp.float32)
    half = NY // 2
    quarter = half // 2
    for zz in range(NZ):
        for j in range(2):
            at = zz * width + j * part
            normed = (raw_all[j, zz].astype(jnp.float32) * shrink * gain[:, at : at + part]).astype(
                jnp.bfloat16
            )
            y0 = half * (zz % 2) + quarter * j
            block = w_in_all[zz // 2, y0 : y0 + quarter].reshape(part, -1)
            projected = projected + jnp.dot(normed, block, preferred_element_type=jnp.float32)

    def rotated(at):
        values = projected[:, at * HD : (at + 1) * HD]
        return values * turns[:, :HD] + pltpu.roll(values, HD // 2, 1) * turns[:, HD:]

    pair = jnp.concatenate([rotated(group), projected[:, (group + 1) * HD :]], axis=1)
    kv_own[:tok, :] = pair[:tok].astype(jnp.bfloat16)
    fresh = pair[tok:]
    valid = lax.broadcasted_iota(jnp.int32, (rows - tok, 1), 0) < rec_count
    kv_own[tok:, :HD] = jnp.where(valid, fresh[:, :HD], fresh[:1, :HD]).astype(jnp.bfloat16)
    kv_own[tok:, HD:] = jnp.where(valid, fresh[:, HD:], ABSENT).astype(jnp.bfloat16)
    kv_run = plane_steps(kv_own, kv_all, sends, local_sems.at[6], 32)
    advance(kv_run)
    runs["k"] = kv_run
    go(KEYING[0])
    drain(cache_run)

    scale = HD**-0.5 * math.log2(math.e)
    few = tok // 2
    for g in range(group):
        turned = (rotated(g) * scale).astype(jnp.bfloat16)
        for h in range(2):
            queries[h, g * few : (g + 1) * few, :] = turned[h * few : (h + 1) * few]
    best[...] = jnp.full_like(best, NEG_FILL)
    accum[...] = jnp.zeros_like(accum)
    span = half * NC

    def update(h, block, mask):
        keys = block[:, :HD]
        values = block[:, HD:].astype(jnp.float32)
        present = values < ABSENT / 2
        values = jnp.concatenate(
            [jnp.where(present, values, 0.0), jnp.where(present, 1.0, 0.0)], axis=1
        ).astype(jnp.bfloat16)
        scores = lax.dot_general(
            queries[h], keys, (((1,), (1,)), ((), ())), preferred_element_type=jnp.float32
        )
        if mask is not None:
            scores = jnp.where(mask, scores, NEG_FILL)
        old = best[h]
        top = jnp.maximum(old, jnp.max(scores, axis=1, keepdims=True))
        factor = jnp.exp2(old - top)
        weights = jnp.exp2(scores - top).astype(jnp.bfloat16)
        best[h] = top
        accum[h] = accum[h] * factor + jnp.dot(weights, values, preferred_element_type=jnp.float32)

    def visit_cache(first, last):
        def visit(step, carry):
            block = cache_all[step // 2, pl.ds(half * (step % 2), half)]
            block = block.reshape(span * cache_rows, 2 * HD)
            for h in range(2):
                update(h, block, None)
            return carry

        lax.fori_loop(first, last, visit, 0)

    def visit_new(h):
        def visit(step, carry):
            xx, y0 = step // 2, half * (step % 2)

            @pl.when(step < s // span)
            def _():
                update(h, kv_all[xx, pl.ds(y0, half)].reshape(span * rows, 2 * HD), None)

            @pl.when(step == s // span)
            def _():
                at = lax.broadcasted_iota(jnp.int32, (1, span * rows), 1)
                row = at % rows
                key_pos = jnp.where(row < tok, (step * span + at // rows) * tok + row, -1)
                query_at = lax.broadcasted_iota(jnp.int32, (group * few, 1), 0)
                query_pos = s * tok + h * few + query_at % few
                update(
                    h,
                    kv_all[xx, pl.ds(y0, half)].reshape(span * rows, 2 * HD),
                    key_pos <= query_pos,
                )

            @pl.when(step > s // span)
            def _():
                block = kv_all[xx, pl.ds(y0, half), :, pl.ds(tok, rows - tok), :]
                update(h, block.reshape(span * (rows - tok), 2 * HD), None)

            return carry

        lax.fori_loop(0, 2 * NX, visit, 0)
        result = accum[h, :, :HD] / accum[h, :, HD:]
        for g in range(group):
            attended[h, :, g * HD : (g + 1) * HD] = result[g * few : (g + 1) * few].astype(
                jnp.bfloat16
            )

    for at, order in enumerate(KEYING[1:]):
        visit_cache(2 * at, 2 * at + 2)
        go(order)
    drain(kv_run)

    odd = z % 2

    def to(k):
        return {"head": (z + k + NZ) % NZ}

    def columns(h, k):
        zz = (z + k + NZ) % NZ
        block = w_out_all[zz // 2, pl.ds(half * (zz % 2), half)].reshape(width, -1)
        return lax.dot_general(
            attended[h], block, (((1,), (1,)), ((), ())), preferred_element_type=jnp.float32
        )

    def share(h, at, value, there, k):
        parts[h, at] = value.astype(jnp.bfloat16)
        return sends.start(parts.at[h, at], there, to(k))

    def share_out(h):
        relays = [
            share(h, 0, columns(h, 4), relayed.at[h, 2], 2 - 4 * odd),
            share(h, 1, columns(h, 3), relayed.at[h, 0], 1),
            share(h, 2, columns(h, -3), relayed.at[h, 1], -1),
        ]
        ends = [
            share(h, 3, columns(h, 1), arrived.at[h, 2], 1),
            share(h, 4, columns(h, -1), arrived.at[h, 3], -1),
        ]
        for at, k in enumerate((2, -2, 0)):
            sums[h, at] = columns(h, k)
        return relays, ends

    def pass_on(h, relays, ends):
        wait_all(relays)
        sums[h, odd] += relayed[h, 2].astype(jnp.float32)
        for at, k in enumerate((2, -2)):
            value = sums[h, at] + relayed[h, at].astype(jnp.float32)
            ends.append(share(h, 5 + at, value, arrived.at[h, at], k))

    def finish(h, ends):
        wait_all(ends)
        mixed = sums[h, 2]
        for at in range(4):
            mixed = mixed + arrived[h, at].astype(jnp.float32)
        out[h * few : (h + 1) * few, :] = mixed.astype(jnp.bfloat16)

    visit_new(0)
    drain(out_run)
    relays, ends = share_out(0)
    visit_new(1)
    pass_on(0, relays, ends)
    relays_last, ends_last = share_out(1)
    finish(0, ends)
    pass_on(1, relays_last, ends_last)
    finish(1, ends_last)
    sends.finish()


def on_device(
    text_rows,
    picture_rows,
    picture_slots,
    norm_gain,
    w_query,
    w_key,
    w_value,
    w_out,
    cache_keys,
    cache_values,
    recompute_rows,
    recompute_slots,
):
    tok, width = text_rows.shape
    rec_count = recompute_rows.shape[0]
    cache_rows = cache_keys.shape[0]
    group = w_query.shape[1] // HD
    rows = tok + 16
    freqs = ROPE_BASE ** (-(np.arange(HD) % (HD // 2)) / (HD // 2))
    plane = (NX, NY, NC)
    bf16, f32 = jnp.bfloat16, jnp.float32
    few = tok // 2
    in_cols = w_query.shape[1] + w_key.shape[1] + w_value.shape[1]
    copies = PIC_COPIES + 4 * PLANE_COPIES + 2 * LINE_COPIES + 14
    vmem = pl.BlockSpec(memory_space=pltpu.VMEM)
    anywhere = pl.BlockSpec(memory_space=pl.ANY)
    given = (
        picture_rows,
        text_rows,
        recompute_rows,
        w_query,
        w_key,
        w_value,
        w_out.T,
        cache_keys,
        cache_values,
    )
    small = (
        norm_gain[None, :],
        jnp.asarray(freqs[None, :], jnp.float32),
        picture_slots[None, :],
        recompute_slots[None, :],
    )
    return pl.pallas_call(
        functools.partial(block_kernel, (tok, width, rec_count, cache_rows, group)),
        out_shape=jax.ShapeDtypeStruct((tok, width), bf16),
        in_specs=[anywhere] * len(given) + [vmem] * len(small),
        out_specs=vmem,
        scratch_shapes=[
            pltpu.VMEM((picture_rows.shape[0], width + HD), bf16),
            pltpu.VMEM((tok, width), bf16),
            pltpu.VMEM((rec_count, width), bf16),
            pltpu.VMEM((w_query.shape[0], in_cols), bf16),
            pltpu.VMEM(w_out.shape[::-1], bf16),
            pltpu.VMEM((cache_rows, 2 * HD), bf16),
            pltpu.VMEM((rows, 2 * HD), f32),
            pltpu.VMEM((cache_rows, 2 * HD), bf16),
            pltpu.VMEM((2, rows, width // 2), bf16),
            pltpu.VMEM((rows, 2 * HD), bf16),
            pltpu.VMEM(plane + (picture_rows.shape[0], width + HD), bf16),
            pltpu.VMEM((2, NZ, rows, width // 2), bf16),
            pltpu.VMEM(plane + (w_query.shape[0], in_cols), bf16),
            pltpu.VMEM(plane + w_out.shape[::-1], bf16),
            pltpu.VMEM(plane + (cache_rows, 2 * HD), bf16),
            pltpu.VMEM(plane + (rows, 2 * HD), bf16),
            pltpu.VMEM((rows, 1), f32),
            pltpu.VMEM((2, group * few, HD), bf16),
            pltpu.VMEM((2, group * few, 1), f32),
            pltpu.VMEM((2, group * few, 2 * HD), f32),
            pltpu.VMEM((2, few, group * HD), bf16),
            pltpu.VMEM((2, 7, few, width), bf16),
            pltpu.VMEM((2, 3, few, width), f32),
            pltpu.VMEM((2, 3, few, width), bf16),
            pltpu.VMEM((2, 4, few, width), bf16),
            pltpu.SemaphoreType.DMA((copies,)),
            pltpu.SemaphoreType.DMA((copies,)),
            pltpu.SemaphoreType.DMA((7,)),
            pltpu.SemaphoreType.DMA((len(given),)),
        ],
        compiler_params=pltpu.CompilerParams(
            collective_id=0, has_side_effects=True, vmem_limit_bytes=56 * 1024 * 1024
        ),
    )(*given, *small)


def solution(mesh):
    return jax.shard_map(
        on_device,
        mesh=mesh,
        in_specs=(
            P("seq", "head"),
            P("seq", "head"),
            P("seq"),
            P(),
            P("seq", "head"),
            P("seq", "head"),
            P("seq", "head"),
            P("head", "seq"),
            P("seq", "head"),
            P("seq", "head"),
            P("seq", "head"),
            P("seq"),
        ),
        out_specs=P("seq", "head"),
        check_vma=False,
    )
```

```python
import functools
import math

import jax
import jax.numpy as jnp
import numpy as np
from jax import lax
from jax.experimental import pallas as pl
from jax.experimental.pallas import tpu as pltpu
from jax.sharding import PartitionSpec as P

D = 4096
HD = 128
NX, NY, NC, NZ = 4, 8, 2, 8
MESH = pl.DeviceIdType.MESH

EPSILON = 1e-05
ROPE_BASE = 1000000.0
NEG_FILL = -1e30
ABSENT = 2.0**127


def place():
    s = lax.axis_index("seq")
    return s // (NY * NC), (s // NC) % NY, s % NC


def seq_of(x, y, c):
    return ((x % NX) * NY + y % NY) * NC + c


class Sends:
    def __init__(self, send_sems, recv_sems):
        self.send_sems, self.recv_sems = send_sems, recv_sems
        self.made, self.settled = [], 0

    def start(self, src, dst, device_id):
        at = len(self.made)
        copy = pltpu.make_async_remote_copy(
            src_ref=src,
            dst_ref=dst,
            send_sem=self.send_sems.at[at],
            recv_sem=self.recv_sems.at[at],
            device_id=device_id,
            device_id_type=MESH,
        )
        copy.start()
        self.made.append(copy)
        return copy

    def settle(self, count=None):
        count = len(self.made) if count is None else count
        for copy in self.made[self.settled : count]:
            copy.wait_send()
        self.settled = count


def wait_all(copies):
    for copy in copies:
        copy.wait_recv()


def ring_near(n, block, source, to, sends):
    return [sends.start(source, block(0), to(d)) for d in (2, -2, 1, -1)]


def ring_far(at, block, to, sends):
    odd = at % 2
    return [
        sends.start(block(-2), block(-2), to(1)),
        sends.start(block(2), block(2), to(-1)),
        sends.start(block(4 * odd - 2), block(4 * odd - 2), to(2 - 4 * odd)),
    ]


NEAR = (-2, 2, -1, 1)
FAR = (-3, 3, 4)


def plane_steps(src, out, sends, local_sem, split):
    x, y, c = place()
    a_rows, b_rows = pl.ds(0, split), pl.ds(split, src.shape[0] - split)
    every_x = pl.ds(0, NX)
    right = {"seq": seq_of(x + 1, y, c)}
    left = {"seq": seq_of(x + NX - 1, y, c)}
    other = {"seq": seq_of(x, y, 1 - c)}

    def col(k):
        return (y + k + NY) % NY

    def up(k):
        return {"seq": seq_of(x, y + k + NY, c)}

    def a_block(k):
        return out.at[every_x, col(k), c, a_rows]

    def b_block(k, xx=x):
        return out.at[xx, col(k), c, b_rows]

    def column(k):
        return out.at[every_x, col(k), c]

    def spread(k, source=None):
        source = b_block(k) if source is None else source
        return [sends.start(source, b_block(k), right), sends.start(source, b_block(k), left)]

    def forward(k):
        odd = col(k) % 2
        block = b_block(k, (x + NX - 1 + 2 * odd) % NX)
        return sends.start(block, block, {"seq": seq_of(x + 1 + 2 * odd, y, c)})

    handed = []

    def hand(ref):
        handed.append(sends.start(ref, ref, other))

    own = pltpu.make_async_copy(src, out.at[x, y, c], local_sem)
    own.start()
    ring_b = ring_near(NY, b_block, src.at[b_rows], up, sends)
    if split:
        along = [
            sends.start(src.at[a_rows], out.at[x, y, c, a_rows], {"seq": seq_of(x + d, y, c)})
            for d in (2, 1, 3)
        ]
    own_spread = spread(0, src.at[b_rows])
    yield
    own.wait()
    if split:
        wait_all(along)
        ring_a = ring_near(NY, a_block, a_block(0), up, sends)
    wait_all(ring_b)
    ring_b = ring_far(y, b_block, up, sends)
    near_spread = [spread(k) for k in NEAR]
    wait_all(own_spread)
    own_forward = forward(0)
    yield
    if split:
        wait_all(ring_a)
        ring_a = ring_far(y, a_block, up, sends)
    wait_all(ring_b)
    far_spread = [spread(k) for k in FAR]
    near_forward = []
    for k, copies in zip(NEAR, near_spread):
        wait_all(copies)
        near_forward.append(forward(k))
    wait_all([own_forward])
    hand(column(0))
    yield
    far_forward = []
    for k, copies in zip(FAR, far_spread):
        wait_all(copies)
        far_forward.append(forward(k))
    if split:
        wait_all(ring_a)
    for k, copy in zip(NEAR, near_forward):
        wait_all([copy])
        hand(column(k))
    yield
    for k, copy in zip(FAR, far_forward):
        wait_all([copy])
        hand(column(k))
    yield
    wait_all(handed)


def line_steps(src, out, sends, local_sem, seen):
    z = lax.axis_index("head")
    odd = z % 2
    up, down = {"head": (z + 1) % NZ}, {"head": (z + NZ - 1) % NZ}

    def block(k):
        return out.at[(z + k + NZ) % NZ]

    own = pltpu.make_async_copy(src, block(0), local_sem)
    own.start()
    ring = [sends.start(src, block(0), up), sends.start(src, block(0), down)]
    own.wait()
    seen(z)
    yield
    for k in range(1, NZ // 2):
        wait_all(ring)
        if k < NZ // 2 - 1:
            ring = [
                sends.start(block(-k), block(-k), up),
                sends.start(block(k), block(k), down),
            ]
        else:
            far = block(k * (2 * odd - 1))
            ring = [sends.start(far, far, {"head": (z + 1 + odd * (NZ - 2)) % NZ})]
        seen((z - k + NZ) % NZ)
        seen((z + k) % NZ)
        yield
    wait_all(ring)
    seen((z + NZ // 2) % NZ)


def greet():
    x, y, c = place()
    z = lax.axis_index("head")
    partners = [{"seq": seq_of(x + d, y, c)} for d in (1, 2, 3)]
    partners += [{"seq": seq_of(x, y + d, c)} for d in (1, 2, NY - 2, NY - 1)]
    partners += [{"seq": seq_of(x, y, 1 - c)}]
    partners += [{"head": (z + d) % NZ} for d in range(1, NZ)]
    barrier = pltpu.get_barrier_semaphore()
    for partner in partners:
        pl.semaphore_signal(barrier, inc=1, device_id=partner, device_id_type=MESH)
    pl.semaphore_wait(barrier, len(partners))


START = "p"
PLACING = "pipipcpip"
LINING = "iclo" "ilci" "locl"
NORMING = "co"
KEYING = ("c", "ko", "ko", "ko", "kko")

OUT_SPLIT = 16
KEY_SPLIT = 32

PIC_COPIES = 39
PLANE_COPIES = 49
LINE_COPIES = 7


def advance(*runs):
    for run in runs:
        next(run, None)


def drain(run):
    for _ in run:
        pass


def block_kernel(dims, *refs):
    tok, width, rec_count, cache_rows, group = dims
    operands, refs = refs[:13], refs[13:]
    hbm_in = operands[:9]
    gain, freqs, slots, rec_slots = operands[9:]
    out, refs = refs[0], refs[1:]
    pics, text, rec, w_in, w_out, cache = refs[:6]
    turns, cache_own, raw, kv_own = refs[6:10]
    pics_all, raw_all, w_in_all, w_out_all, cache_all, kv_all = refs[10:16]
    squares, queries, best, accum, attended = refs[16:21]
    parts, sums, relayed, arrived = refs[21:25]
    send_sems, recv_sems, local_sems, load_sems = refs[25:]

    s = lax.axis_index("seq")
    z = lax.axis_index("head")
    key_cols = HD
    query_cols = group * HD
    places = (
        pics.at[:, pl.ds(0, width)],
        text,
        rec,
        w_in.at[:, pl.ds(0, query_cols)],
        w_in.at[:, pl.ds(query_cols, key_cols)],
        w_in.at[:, pl.ds(query_cols + key_cols, key_cols)],
        w_out,
        cache.at[:, pl.ds(0, key_cols)],
        cache.at[:, pl.ds(key_cols, key_cols)],
    )
    loads = [
        pltpu.make_async_copy(given, here, load_sems.at[i])
        for i, (given, here) in enumerate(zip(hbm_in, places))
    ]
    for load in loads:
        load.start()

    def column(values, count):
        shape = (count, values.shape[1])
        row = lax.broadcasted_iota(jnp.int32, shape, 0)
        lane = lax.broadcasted_iota(jnp.int32, shape, 1)
        return jnp.sum(jnp.where(row == lane, values, 0), axis=1, keepdims=True)

    at_stream = column(slots[...], pics.shape[0])
    lane = lax.broadcasted_iota(jnp.int32, (pics.shape[0], HD), 1)
    marks = jnp.where(lane == 0, at_stream // HD, jnp.where(lane == 1, at_stream % HD, 1))
    pics[:, width:] = marks.astype(jnp.float32).astype(jnp.bfloat16)
    greet()
    for load in loads:
        load.wait()
    sends = Sends(send_sems, recv_sems)
    pic_run = plane_steps(pics, pics_all, sends, local_sems.at[0], 0)
    in_run = plane_steps(w_in, w_in_all, sends, local_sems.at[1], 16)
    out_run = plane_steps(w_out, w_out_all, sends, local_sems.at[2], OUT_SPLIT)
    cache_run = plane_steps(cache_own, cache_all, sends, local_sems.at[3], 16)
    runs = {"p": pic_run, "i": in_run, "o": out_run, "c": cache_run}

    def go(order):
        for name in order:
            advance(*(runs[name] if name == "l" else [runs[name]]))

    go(START)

    cache_at = lax.broadcasted_iota(jnp.int32, (cache_rows, rec_count), 0) + s * cache_rows
    chosen = (cache_at == rec_slots[...]).astype(jnp.float32)
    gone = jnp.max(chosen, axis=1, keepdims=True) > 0.5
    kept_keys = cache[:, :HD].astype(jnp.float32)
    repeat = kept_keys[rec_count : rec_count + 1]
    for r in range(rec_count - 1, -1, -1):
        repeat = jnp.where(gone[r : r + 1], repeat, kept_keys[r : r + 1])
    cache_own[:, :HD] = jnp.where(gone, repeat, kept_keys).astype(jnp.bfloat16)
    cache_own[:, HD:] = jnp.where(gone, ABSENT, cache[:, HD:].astype(jnp.float32)).astype(
        jnp.bfloat16
    )

    rows = raw.shape[1]
    lane = lax.broadcasted_iota(jnp.int32, (1, HD), 1)
    stream_at = lax.broadcasted_iota(jnp.int32, (tok, 1), 0) + (s * tok + NX * NY * NC * cache_rows)
    for first, place_of in ((0, stream_at), (tok, column(rec_slots[...], rows - tok))):
        angles = place_of.astype(jnp.float32) * freqs[...]
        sine = jnp.sin(angles)
        last = first + angles.shape[0]
        turns[first:last, :HD] = jnp.cos(angles)
        turns[first:last, HD:] = jnp.where(lane < HD // 2, -sine, sine)
    go(PLACING)
    drain(pic_run)

    pictures = pics_all[...].reshape(-1, pics.shape[1])
    slot = pictures[:, width : width + 1].astype(jnp.float32) * HD + pictures[
        :, width + 1 : width + 2
    ].astype(jnp.float32)
    position = (s * tok + lax.broadcasted_iota(jnp.int32, (1, tok), 1)).astype(jnp.float32)
    select = (slot == position).astype(jnp.float32).astype(jnp.bfloat16)
    placed = lax.dot_general(
        select, pictures, (((0,), (0,)), ((), ())), preferred_element_type=jnp.float32
    )
    hit = placed[:, width + 2 : width + 3] > 0.5
    stream = jnp.where(hit, placed[:, :width], text[...].astype(jnp.float32)).astype(jnp.bfloat16)
    part = width // 2
    extra = jnp.concatenate(
        [
            rec[...].astype(jnp.float32),
            jnp.zeros((rows - tok - rec_count, width), jnp.float32),
        ],
        axis=0,
    ).astype(jnp.bfloat16)
    squares[...] = jnp.zeros_like(squares)

    def line(j):
        def seen(at):
            wide = raw_all[j, at].astype(jnp.float32)
            squares[...] += jnp.sum(wide * wide, axis=1, keepdims=True)

        return line_steps(raw.at[j], raw_all.at[j], sends, local_sems.at[4 + j], seen)

    lines = [line(j) for j in range(2)]
    runs["l"] = lines
    for j in range(2):
        raw[j, :tok, :] = stream[:, j * part : (j + 1) * part]
        raw[j, tok:, :] = extra[:, j * part : (j + 1) * part]
        advance(lines[j])
    go(LINING)
    drain(lines[0])
    drain(lines[1])

    shrink = lax.rsqrt(squares[...] / D + EPSILON)
    go(NORMING)
    drain(in_run)
    projected = jnp.zeros((rows, w_in.shape[1]), jnp.float32)
    half = NY // 2
    quarter = half // 2
    for zz in range(NZ):
        for j in range(2):
            at = zz * width + j * part
            normed = (raw_all[j, zz].astype(jnp.float32) * shrink * gain[:, at : at + part]).astype(
                jnp.bfloat16
            )
            y0 = half * (zz % 2) + quarter * j
            block = w_in_all[zz // 2, y0 : y0 + quarter].reshape(part, -1)
            projected = projected + jnp.dot(normed, block, preferred_element_type=jnp.float32)

    def rotated(at):
        values = projected[:, at * HD : (at + 1) * HD]
        return values * turns[:, :HD] + pltpu.roll(values, HD // 2, 1) * turns[:, HD:]

    pair = jnp.concatenate([rotated(group), projected[:, (group + 1) * HD :]], axis=1)
    kv_own[:tok, :] = pair[:tok].astype(jnp.bfloat16)
    fresh = pair[tok:]
    valid = lax.broadcasted_iota(jnp.int32, (rows - tok, 1), 0) < rec_count
    kv_own[tok:, :HD] = jnp.where(valid, fresh[:, :HD], fresh[:1, :HD]).astype(jnp.bfloat16)
    kv_own[tok:, HD:] = jnp.where(valid, fresh[:, HD:], ABSENT).astype(jnp.bfloat16)
    early = len(sends.made)
    kv_run = plane_steps(kv_own, kv_all, sends, local_sems.at[6], KEY_SPLIT)
    advance(kv_run)
    runs["k"] = kv_run
    go(KEYING[0])
    drain(cache_run)

    scale = HD**-0.5 * math.log2(math.e)
    few = tok // 2
    for g in range(group):
        turned = (rotated(g) * scale).astype(jnp.bfloat16)
        for h in range(2):
            queries[h, g * few : (g + 1) * few, :] = turned[h * few : (h + 1) * few]
    best[...] = jnp.full_like(best, NEG_FILL)
    accum[...] = jnp.zeros_like(accum)
    span = half * NC

    def update(h, block, mask):
        keys, values = block[:, :HD], block[:, HD:]
        present = values < jnp.bfloat16(ABSENT / 2)
        zero = jnp.zeros_like(values)
        values = jnp.concatenate(
            [jnp.where(present, values, zero), jnp.where(present, zero + 1, zero)], axis=1
        )
        scores = lax.dot_general(
            queries[h], keys, (((1,), (1,)), ((), ())), preferred_element_type=jnp.float32
        )
        if mask is not None:
            scores = jnp.where(mask, scores, NEG_FILL)
        old = best[h]
        top = jnp.maximum(old, jnp.max(scores, axis=1, keepdims=True))
        factor = jnp.exp2(old - top)
        weights = jnp.exp2(scores - top).astype(jnp.bfloat16)
        best[h] = top
        accum[h] = accum[h] * factor + jnp.dot(weights, values, preferred_element_type=jnp.float32)

    def visit_cache(first, last):
        def visit(step, carry):
            block = cache_all[step // 2, pl.ds(half * (step % 2), half)]
            block = block.reshape(span * cache_rows, 2 * HD)
            for h in range(2):
                update(h, block, None)
            return carry

        lax.fori_loop(first, last, visit, 0)

    def visit_new(h):
        def visit(step, carry):
            xx, y0 = step // 2, half * (step % 2)

            @pl.when(step < s // span)
            def _():
                update(h, kv_all[xx, pl.ds(y0, half)].reshape(span * rows, 2 * HD), None)

            @pl.when(step == s // span)
            def _():
                at = lax.broadcasted_iota(jnp.int32, (1, span * rows), 1)
                row = at % rows
                key_pos = jnp.where(row < tok, (step * span + at // rows) * tok + row, -1)
                query_at = lax.broadcasted_iota(jnp.int32, (group * few, 1), 0)
                query_pos = s * tok + h * few + query_at % few
                update(
                    h,
                    kv_all[xx, pl.ds(y0, half)].reshape(span * rows, 2 * HD),
                    key_pos <= query_pos,
                )

            @pl.when(step > s // span)
            def _():
                block = kv_all[xx, pl.ds(y0, half), :, pl.ds(tok, rows - tok), :]
                update(h, block.reshape(span * (rows - tok), 2 * HD), None)

            return carry

        lax.fori_loop(0, 2 * NX, visit, 0)
        result = accum[h, :, :HD] / accum[h, :, HD:]
        for g in range(group):
            attended[h, :, g * HD : (g + 1) * HD] = result[g * few : (g + 1) * few].astype(
                jnp.bfloat16
            )

    for at, order in enumerate(KEYING[1:]):
        visit_cache(2 * at, 2 * at + 2)
        if at < 3:
            sends.settle(early * (at + 1) // 3)
        go(order)
    drain(kv_run)

    odd = z % 2

    def to(k):
        return {"head": (z + k + NZ) % NZ}

    def columns(h, k):
        zz = (z + k + NZ) % NZ
        block = w_out_all[zz // 2, pl.ds(half * (zz % 2), half)].reshape(width, -1)
        return lax.dot_general(
            attended[h], block, (((1,), (1,)), ((), ())), preferred_element_type=jnp.float32
        )

    def share(h, at, value, there, k):
        parts[h, at] = value.astype(jnp.bfloat16)
        return sends.start(parts.at[h, at], there, to(k))

    def share_out(h):
        relays = [
            share(h, 0, columns(h, 4), relayed.at[h, 2], 2 - 4 * odd),
            share(h, 1, columns(h, 3), relayed.at[h, 0], 1),
            share(h, 2, columns(h, -3), relayed.at[h, 1], -1),
        ]
        ends = [
            share(h, 3, columns(h, 1), arrived.at[h, 2], 1),
            share(h, 4, columns(h, -1), arrived.at[h, 3], -1),
        ]
        for at, k in enumerate((2, -2, 0)):
            sums[h, at] = columns(h, k)
        return relays, ends

    def pass_on(h, relays, ends):
        wait_all(relays)
        sums[h, odd] += relayed[h, 2].astype(jnp.float32)
        for at, k in enumerate((2, -2)):
            value = sums[h, at] + relayed[h, at].astype(jnp.float32)
            ends.append(share(h, 5 + at, value, arrived.at[h, at], k))

    def finish(h, ends):
        wait_all(ends)
        mixed = sums[h, 2]
        for at in range(4):
            mixed = mixed + arrived[h, at].astype(jnp.float32)
        out[h * few : (h + 1) * few, :] = mixed.astype(jnp.bfloat16)

    visit_new(0)
    drain(out_run)
    before = len(sends.made)
    relays, ends = share_out(0)
    visit_new(1)
    pass_on(0, relays, ends)
    relays_last, ends_last = share_out(1)
    sends.settle(before)
    finish(0, ends)
    pass_on(1, relays_last, ends_last)
    finish(1, ends_last)
    sends.settle()


def on_device(
    text_rows,
    picture_rows,
    picture_slots,
    norm_gain,
    w_query,
    w_key,
    w_value,
    w_out,
    cache_keys,
    cache_values,
    recompute_rows,
    recompute_slots,
):
    tok, width = text_rows.shape
    rec_count = recompute_rows.shape[0]
    cache_rows = cache_keys.shape[0]
    group = w_query.shape[1] // HD
    rows = tok + 16
    freqs = ROPE_BASE ** (-(np.arange(HD) % (HD // 2)) / (HD // 2))
    plane = (NX, NY, NC)
    bf16, f32 = jnp.bfloat16, jnp.float32
    few = tok // 2
    in_cols = w_query.shape[1] + w_key.shape[1] + w_value.shape[1]
    copies = PIC_COPIES + 4 * PLANE_COPIES + 2 * LINE_COPIES + 14
    vmem = pl.BlockSpec(memory_space=pltpu.VMEM)
    anywhere = pl.BlockSpec(memory_space=pl.ANY)
    given = (
        picture_rows,
        text_rows,
        recompute_rows,
        w_query,
        w_key,
        w_value,
        w_out.T,
        cache_keys,
        cache_values,
    )
    small = (
        norm_gain[None, :],
        jnp.asarray(freqs[None, :], jnp.float32),
        picture_slots[None, :],
        recompute_slots[None, :],
    )
    return pl.pallas_call(
        functools.partial(block_kernel, (tok, width, rec_count, cache_rows, group)),
        out_shape=jax.ShapeDtypeStruct((tok, width), bf16),
        in_specs=[anywhere] * len(given) + [vmem] * len(small),
        out_specs=vmem,
        scratch_shapes=[
            pltpu.VMEM((picture_rows.shape[0], width + HD), bf16),
            pltpu.VMEM((tok, width), bf16),
            pltpu.VMEM((rec_count, width), bf16),
            pltpu.VMEM((w_query.shape[0], in_cols), bf16),
            pltpu.VMEM(w_out.shape[::-1], bf16),
            pltpu.VMEM((cache_rows, 2 * HD), bf16),
            pltpu.VMEM((rows, 2 * HD), f32),
            pltpu.VMEM((cache_rows, 2 * HD), bf16),
            pltpu.VMEM((2, rows, width // 2), bf16),
            pltpu.VMEM((rows, 2 * HD), bf16),
            pltpu.VMEM(plane + (picture_rows.shape[0], width + HD), bf16),
            pltpu.VMEM((2, NZ, rows, width // 2), bf16),
            pltpu.VMEM(plane + (w_query.shape[0], in_cols), bf16),
            pltpu.VMEM(plane + w_out.shape[::-1], bf16),
            pltpu.VMEM(plane + (cache_rows, 2 * HD), bf16),
            pltpu.VMEM(plane + (rows, 2 * HD), bf16),
            pltpu.VMEM((rows, 1), f32),
            pltpu.VMEM((2, group * few, HD), bf16),
            pltpu.VMEM((2, group * few, 1), f32),
            pltpu.VMEM((2, group * few, 2 * HD), f32),
            pltpu.VMEM((2, few, group * HD), bf16),
            pltpu.VMEM((2, 7, few, width), bf16),
            pltpu.VMEM((2, 3, few, width), f32),
            pltpu.VMEM((2, 3, few, width), bf16),
            pltpu.VMEM((2, 4, few, width), bf16),
            pltpu.SemaphoreType.DMA((copies,)),
            pltpu.SemaphoreType.DMA((copies,)),
            pltpu.SemaphoreType.DMA((7,)),
            pltpu.SemaphoreType.DMA((len(given),)),
        ],
        compiler_params=pltpu.CompilerParams(
            collective_id=0, has_side_effects=True, vmem_limit_bytes=56 * 1024 * 1024
        ),
    )(*given, *small)


def solution(mesh):
    return jax.shard_map(
        on_device,
        mesh=mesh,
        in_specs=(
            P("seq", "head"),
            P("seq", "head"),
            P("seq"),
            P(),
            P("seq", "head"),
            P("seq", "head"),
            P("seq", "head"),
            P("head", "seq"),
            P("seq", "head"),
            P("seq", "head"),
            P("seq", "head"),
            P("seq"),
        ),
        out_specs=P("seq", "head"),
        check_vma=False,
    )
```

```python
import functools
import math

import jax
import jax.numpy as jnp
import numpy as np
from jax import lax
from jax.experimental import pallas as pl
from jax.experimental.pallas import tpu as pltpu
from jax.sharding import PartitionSpec as P

D = 4096
HD = 128
NX, NY, NC, NZ = 4, 8, 2, 8
MESH = pl.DeviceIdType.MESH

EPSILON = 1e-05
ROPE_BASE = 1000000.0
NEG_FILL = -1e30
ABSENT = 2.0**127


def place():
    s = lax.axis_index("seq")
    return s // (NY * NC), (s // NC) % NY, s % NC


def seq_of(x, y, c):
    return ((x % NX) * NY + y % NY) * NC + c


class Sends:
    def __init__(self, send_sems, recv_sems):
        self.send_sems, self.recv_sems = send_sems, recv_sems
        self.made, self.settled = [], 0

    def start(self, src, dst, device_id):
        at = len(self.made)
        copy = pltpu.make_async_remote_copy(
            src_ref=src,
            dst_ref=dst,
            send_sem=self.send_sems.at[at],
            recv_sem=self.recv_sems.at[at],
            device_id=device_id,
            device_id_type=MESH,
        )
        copy.start()
        self.made.append(copy)
        return copy

    def settle(self, count=None):
        count = len(self.made) if count is None else count
        for copy in self.made[self.settled : count]:
            copy.wait_send()
        self.settled = count


def wait_all(copies):
    for copy in copies:
        copy.wait_recv()


def ring_near(n, block, source, to, sends):
    return [sends.start(source, block(0), to(d)) for d in (2, -2, 1, -1)]


def ring_far(at, block, to, sends):
    odd = at % 2
    return [
        sends.start(block(-2), block(-2), to(1)),
        sends.start(block(2), block(2), to(-1)),
        sends.start(block(4 * odd - 2), block(4 * odd - 2), to(2 - 4 * odd)),
    ]


NEAR = (-2, 2, -1, 1)
FAR = (-3, 3, 4)


def plane_steps(src, out, sends, local_sem, split):
    x, y, c = place()
    a_rows, b_rows = pl.ds(0, split), pl.ds(split, src.shape[0] - split)
    every_x = pl.ds(0, NX)
    right = {"seq": seq_of(x + 1, y, c)}
    left = {"seq": seq_of(x + NX - 1, y, c)}
    other = {"seq": seq_of(x, y, 1 - c)}

    def col(k):
        return (y + k + NY) % NY

    def up(k):
        return {"seq": seq_of(x, y + k + NY, c)}

    def a_block(k):
        return out.at[every_x, col(k), c, a_rows]

    def b_block(k, xx=x):
        return out.at[xx, col(k), c, b_rows]

    def column(k):
        return out.at[every_x, col(k), c]

    def spread(k, source=None):
        source = b_block(k) if source is None else source
        return [sends.start(source, b_block(k), right), sends.start(source, b_block(k), left)]

    def forward(k):
        odd = col(k) % 2
        block = b_block(k, (x + NX - 1 + 2 * odd) % NX)
        return sends.start(block, block, {"seq": seq_of(x + 1 + 2 * odd, y, c)})

    handed = []

    def hand(ref):
        handed.append(sends.start(ref, ref, other))

    own = pltpu.make_async_copy(src, out.at[x, y, c], local_sem)
    own.start()
    ring_b = ring_near(NY, b_block, src.at[b_rows], up, sends)
    if split:
        along = [
            sends.start(src.at[a_rows], out.at[x, y, c, a_rows], {"seq": seq_of(x + d, y, c)})
            for d in (2, 1, 3)
        ]
    own_spread = spread(0, src.at[b_rows])
    yield
    own.wait()
    if split:
        wait_all(along)
        ring_a = ring_near(NY, a_block, a_block(0), up, sends)
    wait_all(ring_b)
    ring_b = ring_far(y, b_block, up, sends)
    near_spread = [spread(k) for k in NEAR]
    wait_all(own_spread)
    own_forward = forward(0)
    yield
    if split:
        wait_all(ring_a)
        ring_a = ring_far(y, a_block, up, sends)
    wait_all(ring_b)
    far_spread = [spread(k) for k in FAR]
    near_forward = []
    for k, copies in zip(NEAR, near_spread):
        wait_all(copies)
        near_forward.append(forward(k))
    wait_all([own_forward])
    hand(column(0))
    yield
    far_forward = []
    for k, copies in zip(FAR, far_spread):
        wait_all(copies)
        far_forward.append(forward(k))
    if split:
        wait_all(ring_a)
    for k, copy in zip(NEAR, near_forward):
        wait_all([copy])
        hand(column(k))
    yield
    for k, copy in zip(FAR, far_forward):
        wait_all([copy])
        hand(column(k))
    yield
    wait_all(handed)


def line_steps(src, out, sends, local_sem, seen):
    z = lax.axis_index("head")
    odd = z % 2
    up, down = {"head": (z + 1) % NZ}, {"head": (z + NZ - 1) % NZ}

    def block(k):
        return out.at[(z + k + NZ) % NZ]

    own = pltpu.make_async_copy(src, block(0), local_sem)
    own.start()
    ring = [sends.start(src, block(0), up), sends.start(src, block(0), down)]
    own.wait()
    seen(z)
    yield
    for k in range(1, NZ // 2):
        wait_all(ring)
        if k < NZ // 2 - 1:
            ring = [
                sends.start(block(-k), block(-k), up),
                sends.start(block(k), block(k), down),
            ]
        else:
            far = block(k * (2 * odd - 1))
            ring = [sends.start(far, far, {"head": (z + 1 + odd * (NZ - 2)) % NZ})]
        seen((z - k + NZ) % NZ)
        seen((z + k) % NZ)
        yield
    wait_all(ring)
    seen((z + NZ // 2) % NZ)


def greet():
    x, y, c = place()
    z = lax.axis_index("head")
    partners = [{"seq": seq_of(x + d, y, c)} for d in (1, 2, 3)]
    partners += [{"seq": seq_of(x, y + d, c)} for d in (1, 2, NY - 2, NY - 1)]
    partners += [{"seq": seq_of(x, y, 1 - c)}]
    partners += [{"head": (z + d) % NZ} for d in range(1, NZ)]
    barrier = pltpu.get_barrier_semaphore()
    for partner in partners:
        pl.semaphore_signal(barrier, inc=1, device_id=partner, device_id_type=MESH)
    pl.semaphore_wait(barrier, len(partners))


START = "p"
PLACING = "pipipcpip"
LINING = "iclo" "ilci" "locl"
NORMING = "co"
KEYING = ("c", "ko", "ko", "ko", "kko")

OUT_SPLIT = 16
KEY_SPLIT = 32

PIC_COPIES = 39
PLANE_COPIES = 49
LINE_COPIES = 7


def advance(*runs):
    for run in runs:
        next(run, None)


def drain(run):
    for _ in run:
        pass


def block_kernel(dims, *refs):
    tok, width, rec_count, cache_rows, group = dims
    operands, refs = refs[:13], refs[13:]
    hbm_in = operands[:9]
    gain, freqs, slots, rec_slots = operands[9:]
    out, refs = refs[0], refs[1:]
    pics, text, rec, w_in, w_out, cache = refs[:6]
    turns, cache_own, raw, kv_own = refs[6:10]
    pics_all, raw_all, w_in_all, w_out_all, cache_all, kv_all = refs[10:16]
    squares, queries, best, accum, attended = refs[16:21]
    parts, sums, relayed, arrived = refs[21:25]
    send_sems, recv_sems, local_sems, load_sems = refs[25:]

    s = lax.axis_index("seq")
    z = lax.axis_index("head")
    key_cols = HD
    query_cols = group * HD
    places = (
        pics.at[:, pl.ds(0, width)],
        text,
        rec,
        w_in.at[:, pl.ds(0, query_cols)],
        w_in.at[:, pl.ds(query_cols, key_cols)],
        w_in.at[:, pl.ds(query_cols + key_cols, key_cols)],
        w_out,
        cache.at[:, pl.ds(0, key_cols)],
        cache.at[:, pl.ds(key_cols, key_cols)],
    )
    loads = [
        pltpu.make_async_copy(given, here, load_sems.at[i])
        for i, (given, here) in enumerate(zip(hbm_in, places))
    ]
    for load in loads:
        load.start()

    def column(values, count):
        shape = (count, values.shape[1])
        row = lax.broadcasted_iota(jnp.int32, shape, 0)
        lane = lax.broadcasted_iota(jnp.int32, shape, 1)
        return jnp.sum(jnp.where(row == lane, values, 0), axis=1, keepdims=True)

    at_stream = column(slots[...], pics.shape[0])
    lane = lax.broadcasted_iota(jnp.int32, (pics.shape[0], HD), 1)
    marks = jnp.where(lane == 0, at_stream // HD, jnp.where(lane == 1, at_stream % HD, 1))
    pics[:, width:] = marks.astype(jnp.float32).astype(jnp.bfloat16)
    greet()
    for load in loads:
        load.wait()
    sends = Sends(send_sems, recv_sems)
    pic_run = plane_steps(pics, pics_all, sends, local_sems.at[0], 0)
    in_run = plane_steps(w_in, w_in_all, sends, local_sems.at[1], 16)
    out_run = plane_steps(w_out, w_out_all, sends, local_sems.at[2], OUT_SPLIT)
    cache_run = plane_steps(cache_own, cache_all, sends, local_sems.at[3], 16)
    runs = {"p": pic_run, "i": in_run, "o": out_run, "c": cache_run}

    def go(order):
        for name in order:
            advance(*(runs[name] if name == "l" else [runs[name]]))

    go(START)

    cache_at = lax.broadcasted_iota(jnp.int32, (cache_rows, rec_count), 0) + s * cache_rows
    chosen = (cache_at == rec_slots[...]).astype(jnp.float32)
    gone = jnp.max(chosen, axis=1, keepdims=True) > 0.5
    kept_keys = cache[:, :HD].astype(jnp.float32)
    repeat = kept_keys[rec_count : rec_count + 1]
    for r in range(rec_count - 1, -1, -1):
        repeat = jnp.where(gone[r : r + 1], repeat, kept_keys[r : r + 1])
    cache_own[:, :HD] = jnp.where(gone, repeat, kept_keys).astype(jnp.bfloat16)
    cache_own[:, HD:] = jnp.where(gone, ABSENT, cache[:, HD:].astype(jnp.float32)).astype(
        jnp.bfloat16
    )

    rows = raw.shape[1]
    lane = lax.broadcasted_iota(jnp.int32, (1, HD), 1)
    stream_at = lax.broadcasted_iota(jnp.int32, (tok, 1), 0) + (s * tok + NX * NY * NC * cache_rows)
    for first, place_of in ((0, stream_at), (tok, column(rec_slots[...], rows - tok))):
        angles = place_of.astype(jnp.float32) * freqs[...]
        sine = jnp.sin(angles)
        last = first + angles.shape[0]
        turns[first:last, :HD] = jnp.cos(angles)
        turns[first:last, HD:] = jnp.where(lane < HD // 2, -sine, sine)
    go(PLACING)
    drain(pic_run)

    pictures = pics_all[...].reshape(-1, pics.shape[1])
    slot = pictures[:, width : width + 1].astype(jnp.float32) * HD + pictures[
        :, width + 1 : width + 2
    ].astype(jnp.float32)
    position = (s * tok + lax.broadcasted_iota(jnp.int32, (1, tok), 1)).astype(jnp.float32)
    select = (slot == position).astype(jnp.float32).astype(jnp.bfloat16)
    placed = lax.dot_general(
        select, pictures, (((0,), (0,)), ((), ())), preferred_element_type=jnp.float32
    )
    hit = placed[:, width + 2 : width + 3] > 0.5
    stream = jnp.where(hit, placed[:, :width], text[...].astype(jnp.float32)).astype(jnp.bfloat16)
    part = width // 2
    extra = jnp.concatenate(
        [
            rec[...].astype(jnp.float32),
            jnp.zeros((rows - tok - rec_count, width), jnp.float32),
        ],
        axis=0,
    ).astype(jnp.bfloat16)
    squares[...] = jnp.zeros_like(squares)

    def line(j):
        def seen(at):
            wide = raw_all[j, at].astype(jnp.float32)
            squares[...] += jnp.sum(wide * wide, axis=1, keepdims=True)

        return line_steps(raw.at[j], raw_all.at[j], sends, local_sems.at[4 + j], seen)

    lines = [line(j) for j in range(2)]
    runs["l"] = lines
    for j in range(2):
        raw[j, :tok, :] = stream[:, j * part : (j + 1) * part]
        raw[j, tok:, :] = extra[:, j * part : (j + 1) * part]
        advance(lines[j])
    go(LINING)
    drain(lines[0])
    drain(lines[1])

    shrink = lax.rsqrt(squares[...] / D + EPSILON)
    go(NORMING)
    drain(in_run)
    projected = jnp.zeros((rows, w_in.shape[1]), jnp.float32)
    half = NY // 2
    quarter = half // 2
    for zz in range(NZ):
        for j in range(2):
            at = zz * width + j * part
            normed = (raw_all[j, zz].astype(jnp.float32) * shrink * gain[:, at : at + part]).astype(
                jnp.bfloat16
            )
            y0 = half * (zz % 2) + quarter * j
            block = w_in_all[zz // 2, y0 : y0 + quarter].reshape(part, -1)
            projected = projected + jnp.dot(normed, block, preferred_element_type=jnp.float32)

    def rotated(at):
        values = projected[:, at * HD : (at + 1) * HD]
        return values * turns[:, :HD] + pltpu.roll(values, HD // 2, 1) * turns[:, HD:]

    pair = jnp.concatenate([rotated(group), projected[:, (group + 1) * HD :]], axis=1)
    kv_own[:tok, :] = pair[:tok].astype(jnp.bfloat16)
    fresh = pair[tok:]
    valid = lax.broadcasted_iota(jnp.int32, (rows - tok, 1), 0) < rec_count
    kv_own[tok:, :HD] = jnp.where(valid, fresh[:, :HD], fresh[:1, :HD]).astype(jnp.bfloat16)
    kv_own[tok:, HD:] = jnp.where(valid, fresh[:, HD:], ABSENT).astype(jnp.bfloat16)
    early = len(sends.made)
    kv_run = plane_steps(kv_own, kv_all, sends, local_sems.at[6], KEY_SPLIT)
    advance(kv_run)
    runs["k"] = kv_run
    go(KEYING[0])
    drain(cache_run)

    scale = HD**-0.5 * math.log2(math.e)
    few = tok // 2
    for g in range(group):
        turned = (rotated(g) * scale).astype(jnp.bfloat16)
        for h in range(2):
            queries[h, g * few : (g + 1) * few, :] = turned[h * few : (h + 1) * few]
    best[...] = jnp.full_like(best, NEG_FILL)
    accum[...] = jnp.zeros_like(accum)
    span = half * NC

    def update(h, block, mask):
        keys, values = block[:, :HD], block[:, HD:]
        present = values < jnp.bfloat16(ABSENT / 2)
        zero = jnp.zeros_like(values)
        values = jnp.concatenate(
            [jnp.where(present, values, zero), jnp.where(present, zero + 1, zero)], axis=1
        )
        scores = lax.dot_general(
            queries[h], keys, (((1,), (1,)), ((), ())), preferred_element_type=jnp.float32
        )
        if mask is not None:
            scores = jnp.where(mask, scores, NEG_FILL)
        old = best[h]
        top = jnp.maximum(old, jnp.max(scores, axis=1, keepdims=True))
        factor = jnp.exp2(old - top)
        weights = jnp.exp2(scores - top).astype(jnp.bfloat16)
        best[h] = top
        accum[h] = accum[h] * factor + jnp.dot(weights, values, preferred_element_type=jnp.float32)

    def visit_cache(first, last):
        def visit(step, carry):
            block = cache_all[step // 2, pl.ds(half * (step % 2), half)]
            block = block.reshape(span * cache_rows, 2 * HD)
            for h in range(2):
                update(h, block, None)
            return carry

        lax.fori_loop(first, last, visit, 0)

    def visit_new(h, first, last):
        def visit(step, carry):
            xx, y0 = step // 2, half * (step % 2)

            @pl.when(step < s // span)
            def _():
                update(h, kv_all[xx, pl.ds(y0, half)].reshape(span * rows, 2 * HD), None)

            @pl.when(step == s // span)
            def _():
                at = lax.broadcasted_iota(jnp.int32, (1, span * rows), 1)
                row = at % rows
                key_pos = jnp.where(row < tok, (step * span + at // rows) * tok + row, -1)
                query_at = lax.broadcasted_iota(jnp.int32, (group * few, 1), 0)
                query_pos = s * tok + h * few + query_at % few
                update(
                    h,
                    kv_all[xx, pl.ds(y0, half)].reshape(span * rows, 2 * HD),
                    key_pos <= query_pos,
                )

            @pl.when(step > s // span)
            def _():
                block = kv_all[xx, pl.ds(y0, half), :, pl.ds(tok, rows - tok), :]
                update(h, block.reshape(span * (rows - tok), 2 * HD), None)

            return carry

        lax.fori_loop(first, last, visit, 0)

    def close(h):
        result = accum[h, :, :HD] / accum[h, :, HD:]
        for g in range(group):
            attended[h, :, g * HD : (g + 1) * HD] = result[g * few : (g + 1) * few].astype(
                jnp.bfloat16
            )

    for at, order in enumerate(KEYING[1:]):
        visit_cache(2 * at, 2 * at + 2)
        if at < 3:
            sends.settle(early * (at + 1) // 3)
        go(order)
    drain(kv_run)

    odd = z % 2

    def to(k):
        return {"head": (z + k + NZ) % NZ}

    def columns(h, k):
        zz = (z + k + NZ) % NZ
        block = w_out_all[zz // 2, pl.ds(half * (zz % 2), half)].reshape(width, -1)
        return lax.dot_general(
            attended[h], block, (((1,), (1,)), ((), ())), preferred_element_type=jnp.float32
        )

    def share(h, at, value, there, k):
        parts[h, at] = value.astype(jnp.bfloat16)
        return sends.start(parts.at[h, at], there, to(k))

    def share_out(h):
        relays = [
            share(h, 0, columns(h, 4), relayed.at[h, 2], 2 - 4 * odd),
            share(h, 1, columns(h, 3), relayed.at[h, 0], 1),
            share(h, 2, columns(h, -3), relayed.at[h, 1], -1),
        ]
        ends = [
            share(h, 3, columns(h, 1), arrived.at[h, 2], 1),
            share(h, 4, columns(h, -1), arrived.at[h, 3], -1),
        ]
        for at, k in enumerate((2, -2, 0)):
            sums[h, at] = columns(h, k)
        return relays, ends

    def pass_on(h, relays, ends):
        wait_all(relays)
        sums[h, odd] += relayed[h, 2].astype(jnp.float32)
        for at, k in enumerate((2, -2)):
            value = sums[h, at] + relayed[h, at].astype(jnp.float32)
            ends.append(share(h, 5 + at, value, arrived.at[h, at], k))

    def finish(h, ends):
        wait_all(ends)
        mixed = sums[h, 2]
        for at in range(4):
            mixed = mixed + arrived[h, at].astype(jnp.float32)
        out[h * few : (h + 1) * few, :] = mixed.astype(jnp.bfloat16)

    visit_new(0, 0, 2 * NX)
    close(0)
    drain(out_run)
    before = len(sends.made)
    relays, ends = share_out(0)
    visit_new(1, 0, 2 * NX - 2)
    pass_on(0, relays, ends)
    visit_new(1, 2 * NX - 2, 2 * NX)
    close(1)
    relays_last, ends_last = share_out(1)
    sends.settle(before)
    finish(0, ends)
    pass_on(1, relays_last, ends_last)
    finish(1, ends_last)
    sends.settle()


def on_device(
    text_rows,
    picture_rows,
    picture_slots,
    norm_gain,
    w_query,
    w_key,
    w_value,
    w_out,
    cache_keys,
    cache_values,
    recompute_rows,
    recompute_slots,
):
    tok, width = text_rows.shape
    rec_count = recompute_rows.shape[0]
    cache_rows = cache_keys.shape[0]
    group = w_query.shape[1] // HD
    rows = tok + 16
    freqs = ROPE_BASE ** (-(np.arange(HD) % (HD // 2)) / (HD // 2))
    plane = (NX, NY, NC)
    bf16, f32 = jnp.bfloat16, jnp.float32
    few = tok // 2
    in_cols = w_query.shape[1] + w_key.shape[1] + w_value.shape[1]
    copies = PIC_COPIES + 4 * PLANE_COPIES + 2 * LINE_COPIES + 14
    vmem = pl.BlockSpec(memory_space=pltpu.VMEM)
    anywhere = pl.BlockSpec(memory_space=pl.ANY)
    given = (
        picture_rows,
        text_rows,
        recompute_rows,
        w_query,
        w_key,
        w_value,
        w_out.T,
        cache_keys,
        cache_values,
    )
    small = (
        norm_gain[None, :],
        jnp.asarray(freqs[None, :], jnp.float32),
        picture_slots[None, :],
        recompute_slots[None, :],
    )
    return pl.pallas_call(
        functools.partial(block_kernel, (tok, width, rec_count, cache_rows, group)),
        out_shape=jax.ShapeDtypeStruct((tok, width), bf16),
        in_specs=[anywhere] * len(given) + [vmem] * len(small),
        out_specs=vmem,
        scratch_shapes=[
            pltpu.VMEM((picture_rows.shape[0], width + HD), bf16),
            pltpu.VMEM((tok, width), bf16),
            pltpu.VMEM((rec_count, width), bf16),
            pltpu.VMEM((w_query.shape[0], in_cols), bf16),
            pltpu.VMEM(w_out.shape[::-1], bf16),
            pltpu.VMEM((cache_rows, 2 * HD), bf16),
            pltpu.VMEM((rows, 2 * HD), f32),
            pltpu.VMEM((cache_rows, 2 * HD), bf16),
            pltpu.VMEM((2, rows, width // 2), bf16),
            pltpu.VMEM((rows, 2 * HD), bf16),
            pltpu.VMEM(plane + (picture_rows.shape[0], width + HD), bf16),
            pltpu.VMEM((2, NZ, rows, width // 2), bf16),
            pltpu.VMEM(plane + (w_query.shape[0], in_cols), bf16),
            pltpu.VMEM(plane + w_out.shape[::-1], bf16),
            pltpu.VMEM(plane + (cache_rows, 2 * HD), bf16),
            pltpu.VMEM(plane + (rows, 2 * HD), bf16),
            pltpu.VMEM((rows, 1), f32),
            pltpu.VMEM((2, group * few, HD), bf16),
            pltpu.VMEM((2, group * few, 1), f32),
            pltpu.VMEM((2, group * few, 2 * HD), f32),
            pltpu.VMEM((2, few, group * HD), bf16),
            pltpu.VMEM((2, 7, few, width), bf16),
            pltpu.VMEM((2, 3, few, width), f32),
            pltpu.VMEM((2, 3, few, width), bf16),
            pltpu.VMEM((2, 4, few, width), bf16),
            pltpu.SemaphoreType.DMA((copies,)),
            pltpu.SemaphoreType.DMA((copies,)),
            pltpu.SemaphoreType.DMA((7,)),
            pltpu.SemaphoreType.DMA((len(given),)),
        ],
        compiler_params=pltpu.CompilerParams(
            collective_id=0, has_side_effects=True, vmem_limit_bytes=56 * 1024 * 1024
        ),
    )(*given, *small)


def solution(mesh):
    return jax.shard_map(
        on_device,
        mesh=mesh,
        in_specs=(
            P("seq", "head"),
            P("seq", "head"),
            P("seq"),
            P(),
            P("seq", "head"),
            P("seq", "head"),
            P("seq", "head"),
            P("head", "seq"),
            P("seq", "head"),
            P("seq", "head"),
            P("seq", "head"),
            P("seq"),
        ),
        out_specs=P("seq", "head"),
        check_vma=False,
    )
```
